32 devices in a mesh: rep: 2 (over x), grp: 4 (over z), tp: 4 (over y, core).
Axes of the slice: x: 2, y: 2, z: 4, core: 2. Of those that a mesh axis runs over, the one named last changes fastest.
Arguments:
- x_in: bfloat16 [4, 8, 128, 1280], P(None, ('rep', 'grp'), None, 'tp'), parts along dimension 1, may hold values from -6 to 6
- taps: bfloat16 [4, 8, 128, 6400], P(None, ('rep', 'grp'), None, 'tp'), parts along dimension 1, may hold values from -6 to 6
- ln_gain: float32 [1280], replicated, may hold values from 0.1 to 1.9
- ln_bias: float32 [1280], replicated, may hold values from -3 to 3
- w_up: bfloat16 [1280, 5120], P(None, 'tp'), may hold values from -0.15625 to 0.15625
- b_up: float32 [5120], P('tp'), may hold values from -3 to 3
- w_down: bfloat16 [5120, 1280], P('tp'), may hold values from -0.078125 to 0.078125
- b_down: float32 [1280], P('tp'), may hold values from -3 to 3
- kv_w_out: bfloat16 [1280, 2048], P('tp'), may hold values from -0.0625 to 0.0625
- kv_w_taps: bfloat16 [6400, 2048], P('tp'), may hold values from -0.09375 to 0.09375
- k_gain: float32 [128], replicated, may hold values from 1 to 2.5
- q_gain: float32 [128], replicated, may hold values from 1 to 2.5
- queries: bfloat16 [4096, 8192], P(('rep', 'grp'), 'tp'), parts along dimension 0, may hold values from -6 to 6
- tiles_per_request: int32 [16], P('rep'), parts along dimension 0, may hold values from 1 to 4, as said below
- owner: int32 [16], P('rep'), parts along dimension 0, may hold values from 0 to 3, as said below
- text_per_request: int32 [16], P('rep'), parts along dimension 0, may hold values from 64 to 256, as said below
Outputs:
- attended: bfloat16 [4096, 8192], P(('rep', 'grp'), 'tp'), parts along dimension 0
The draws below stay inside these ranges and needn't reach their ends.
There are 2 independent parts, one for each index of `rep`. The reference program is written for one: setup_inputs(seed, part) draws one part's arguments, and reference() takes and returns one part's arrays. A program takes and returns all parts, laid end to end along the dimension named above; an argument that names none is the same for every part. Nothing has to cross between parts.
Inputs may be any that keep to these rules, and one draw needn't show every extreme that they name: `owner`: each group owns exactly 2 requests. `tiles_per_request`: the tiles of all requests sum to 16; the tiles of one group's requests sum to at most 8, and some group has exactly 8. `text_per_request`: the text tokens of one group's requests sum to at most 512, and some group has exactly 512.
All inputs are finite; a program needn't handle non-finite values.
Results may differ from the reference program's by a relative error of at most 0.04.
Values may be sent and summed in bfloat16 or wider, within the bound.
A program may use at most 128 MiB of HBM per device.

```python
import math
import jax
import jax.numpy as jnp
from jax import lax

DV = 1280
MLPV = 5120
TAPS = 5
QH = 64
KVH = 8
HD = 128
TILE_ROWS = 128
TEXT_G = 512
TILES_ENC = 4
MAXT = 4
REQ_G = 2
FEAT = 7680
KVW = 2048
QW = 8192
TILES = 16
NREQ = 8
CAP = 8
N_GRP = 4
N_TP = 4


def owner_table(key):
    shuffled = jax.random.permutation(jax.random.fold_in(key, 101), NREQ)
    return (shuffled // REQ_G).astype(jnp.int32)


def chosen_group(key, salt):
    return jax.random.randint(jax.random.fold_in(key, salt), (), 0, N_GRP).astype(jnp.int32)


def draw_owner(key, part):
    return owner_table(key)


def draw_tiles_per_request(key, part):
    owners = owner_table(key)
    forced = owners == chosen_group(key, 202)
    extra_total = TILES - CAP - (NREQ - REQ_G)
    priority = jax.random.randint(jax.random.fold_in(key, 303), (max(extra_total, 1), NREQ), 0, 1 << 20)
    request_ids = jnp.arange(NREQ, dtype=jnp.int32)

    def add_one(step_index, extra):
        eligible = jnp.logical_not(forced) & (extra < MAXT - 1)
        ranked = jnp.where(eligible, priority[step_index], -1)
        picked = jnp.argmax(ranked).astype(jnp.int32)
        return extra + (request_ids == picked).astype(jnp.int32)
    extra = lax.fori_loop(0, extra_total, add_one, jnp.zeros((NREQ,), jnp.int32))
    return jnp.where(forced, MAXT, 1 + extra).astype(jnp.int32)


def draw_text_per_request(key, part):
    owners = owner_table(key)
    forced = owners == chosen_group(key, 404)
    base_counts = jax.random.randint(jax.random.fold_in(key, 505), (NREQ,), TEXT_G // 8, TEXT_G // 2 + 1)
    return jnp.where(forced, TEXT_G // 2, base_counts).astype(jnp.int32)


def with_spikes(values, rng, source, target, shards_of, factor):
    def block_of(dim):
        return (jnp.arange(values.shape[dim]) // (values.shape[dim] // shards_of)).reshape((-1,) + (1,) * (values.ndim - 1 - dim))

    near = jax.random.permutation(rng, shards_of)[block_of(target)]
    other_side = (block_of(target) + shards_of // 2) % shards_of
    return jnp.where((block_of(source) == near) | (block_of(source) == other_side), factor * values, values)


def steps_of(key, shape, split, least, high):
    def one(dim, parts):
        steps = jax.random.uniform(jax.random.fold_in(jax.random.fold_in(key, 6), dim), (parts,), jnp.float32, least / len(split), high / len(split))
        return jnp.repeat(jnp.exp(steps), shape[dim] // parts).reshape((-1,) + (1,) * (len(shape) - dim - 1))

    loudness = one(*split[0])
    for cut in split[1:]:
        loudness = loudness * one(*cut)
    return loudness


def gaussian(rng, shape, deviation, limit, split=(), kind=jnp.bfloat16):
    values = deviation * jax.random.normal(rng, shape, jnp.float32)
    if split:
        values = values * steps_of(rng, shape, split, -0.22, 0.18)
    return jnp.clip(values, -limit, limit).astype(kind)


def bell_draw_with(rng, dims, width, limit, shards, heavy, kind=jnp.bfloat16):
    values = width * jax.random.normal(rng, dims, jnp.float32)
    if shards:
        values = values * steps_of(rng, dims, shards, -0.22, 0.18)
    return jnp.clip(with_spikes(values, jax.random.fold_in(rng, 3), *heavy), -limit, limit).astype(kind)


def setup_inputs(seed: int = 0, part: int = 0) -> dict:
    keys = jax.random.split(jax.random.key(seed), 17)
    part_splits = jax.random.split(jax.random.fold_in(keys[16], part), 17)
    return {
        "x_in": gaussian(part_splits[0], (TILES_ENC, N_GRP, TILE_ROWS, DV), 1.0, 6.0, ((1, 4), (3, 4))),
        "taps": gaussian(part_splits[1], (TILES_ENC, N_GRP, TILE_ROWS, DV * TAPS), 1.0, 6.0, ((1, 4), (3, 4))),
        "ln_gain": jnp.clip(1.0 + 0.18 * jax.random.normal(keys[2], (DV,), jnp.float32), 0.1, 1.9),
        "ln_bias": gaussian(keys[3], (DV,), 0.5, 3.0, (), jnp.float32),
        "w_up": gaussian(keys[4], (DV, MLPV), DV ** -0.5, 0.15625, ((1, 4),)),
        "b_up": gaussian(keys[5], (MLPV,), 0.5, 3.0, ((0, 4),), jnp.float32),
        "w_down": gaussian(keys[6], (MLPV, DV), MLPV ** -0.5, 0.078125, ((0, 4),)),
        "b_down": gaussian(keys[7], (DV,), 0.5, 3.0, ((0, 4),), jnp.float32),
        "kv_w_out": gaussian(keys[8], (DV, KVW), FEAT ** -0.5, 0.0625, ((0, 4),)),
        "kv_w_taps": bell_draw_with(keys[9], (DV * TAPS, KVW), FEAT ** -0.5, 0.09375, ((0, 4),), (0, 1, 4, 2.0)),
        "k_gain": jnp.clip(jnp.exp(jax.random.uniform(keys[10], (HD,), jnp.float32, math.log(1.0), math.log(2.5))), 1.0, 2.5),
        "q_gain": jnp.clip(jnp.exp(jax.random.uniform(keys[11], (HD,), jnp.float32, math.log(1.0), math.log(2.5))), 1.0, 2.5),
        "queries": gaussian(part_splits[12], (N_GRP * TEXT_G, QW), 1.0, 6.0, ((0, 4), (1, 4))),
        "tiles_per_request": draw_tiles_per_request(jax.random.fold_in(jax.random.fold_in(keys[16], part), 71), part),
        "owner": draw_owner(jax.random.fold_in(jax.random.fold_in(keys[16], part), 71), part),
        "text_per_request": draw_text_per_request(jax.random.fold_in(jax.random.fold_in(keys[16], part), 71), part),
    }


epsilon = 1e-05

def layer_norm(row_block, ln_gain, ln_bias):
    values = row_block.astype(jnp.float32)
    average = lax.optimization_barrier(jnp.mean(values, axis=-1, keepdims=True))
    centered = values - average
    variance = lax.optimization_barrier(jnp.mean(centered * centered, axis=-1, keepdims=True))
    return (centered * lax.rsqrt(variance + epsilon) * ln_gain + ln_bias).astype(jnp.bfloat16)

def head_norm(values, head_gain):
    square = lax.optimization_barrier(jnp.mean(values * values, axis=-1, keepdims=True))
    return values * lax.rsqrt(square + epsilon) * head_gain

def group_layout(tiles_per_request, owner, text_per_request, group_count):
    request_count = owner.shape[0]
    request_ids = jnp.arange(request_count, dtype=jnp.int32)
    group_ids = jnp.arange(group_count, dtype=jnp.int32)
    member = owner[None, :] == group_ids[:, None]
    first_req = lax.optimization_barrier(jnp.min(jnp.where(member, request_ids[None, :], request_count), axis=1))
    second_req = lax.optimization_barrier(jnp.max(jnp.where(member, request_ids[None, :], -1), axis=1))
    pick_first = request_ids[None, :] == first_req[:, None]
    pick_second = request_ids[None, :] == second_req[:, None]
    tiles_first = lax.optimization_barrier(jnp.sum(jnp.where(pick_first, tiles_per_request[None, :], 0), axis=1)).astype(jnp.int32)
    tiles_second = lax.optimization_barrier(jnp.sum(jnp.where(pick_second, tiles_per_request[None, :], 0), axis=1)).astype(jnp.int32)
    text_first = lax.optimization_barrier(jnp.sum(jnp.where(pick_first, text_per_request[None, :], 0), axis=1)).astype(jnp.int32)
    text_second = lax.optimization_barrier(jnp.sum(jnp.where(pick_second, text_per_request[None, :], 0), axis=1)).astype(jnp.int32)
    tiles_both = (tiles_first + tiles_second).astype(jnp.int32)
    text_both = (text_first + text_second).astype(jnp.int32)
    offsets = (jnp.cumsum(tiles_both) - tiles_both).astype(jnp.int32)
    return (tiles_first, tiles_both, offsets, text_first, text_both)

def slot_label(position, first_count, both_count):
    return jnp.where(position < first_count, 0, jnp.where(position < both_count, 1, -1)).astype(jnp.int32)

def reference(x_in, taps, ln_gain, ln_bias, w_up, b_up, w_down, b_down, kv_w_out, kv_w_taps, k_gain, q_gain, queries, tiles_per_request, owner, text_per_request):
    token_count = TILES * TILE_ROWS
    token_rows = x_in.reshape(token_count, DV)
    normed = layer_norm(token_rows, ln_gain, ln_bias)
    hidden = jax.nn.gelu(jnp.dot(normed, w_up, preferred_element_type=jnp.float32) + b_up, approximate=False).astype(jnp.bfloat16)
    encoded = (token_rows.astype(jnp.float32) + jnp.dot(hidden, w_down, preferred_element_type=jnp.float32) + b_down).astype(jnp.bfloat16)
    tap_rows = taps.reshape(token_count, DV * TAPS)
    out_block = DV // N_TP
    tap_block = DV * TAPS // N_TP
    kv_total = jnp.zeros((token_count, KVW), jnp.float32)
    for block_index in range(N_TP):
        part_out = jnp.dot(encoded[:, block_index * out_block:(block_index + 1) * out_block], kv_w_out[block_index * out_block:(block_index + 1) * out_block], preferred_element_type=jnp.float32)
        part_tap = jnp.dot(tap_rows[:, block_index * tap_block:(block_index + 1) * tap_block], kv_w_taps[block_index * tap_block:(block_index + 1) * tap_block], preferred_element_type=jnp.float32)
        rounded = lax.optimization_barrier((part_out + part_tap).astype(jnp.bfloat16))
        kv_total = kv_total + rounded.astype(jnp.float32)
    kv_total = kv_total.reshape(TILES, TILE_ROWS, KVH, 2, HD)
    key_rows = head_norm(kv_total[:, :, :, 0, :], k_gain).astype(jnp.bfloat16)
    value_rows = kv_total[:, :, :, 1, :].astype(jnp.bfloat16)
    tiles_first, tiles_both, offsets, text_first, text_both = group_layout(tiles_per_request, owner, text_per_request, N_GRP)
    group_size = QH // KVH
    query_view = queries.reshape(N_GRP, TEXT_G, KVH, group_size, HD).astype(jnp.float32)
    query_rows = head_norm(query_view, q_gain).astype(jnp.bfloat16)
    slot_ids = jnp.arange(CAP, dtype=jnp.int32)
    text_ids = jnp.arange(TEXT_G, dtype=jnp.int32)
    scale = 1.0 / math_sqrt(HD)

    def per_group(item):
        query_group, first_count, both_count, offset, text_one, text_two = item
        tile_index = jnp.clip(offset + slot_ids, 0, TILES - 1).astype(jnp.int32)
        key_group = jnp.take(key_rows, tile_index, axis=0).reshape(CAP * TILE_ROWS, KVH, HD)
        value_group = jnp.take(value_rows, tile_index, axis=0).reshape(CAP * TILE_ROWS, KVH, HD)
        key_label = jnp.repeat(slot_label(slot_ids, first_count, both_count), TILE_ROWS)
        text_label = slot_label(text_ids, text_one, text_two)
        allowed = (text_label[:, None] == key_label[None, :]) & (text_label[:, None] >= 0)
        live_rows = text_label >= 0

        def per_head(head_item):
            query_head, key_head, value_head = head_item
            scores = jnp.einsum('tgd,sd->tgs', query_head.astype(jnp.float32), key_head.astype(jnp.float32)) * scale
            weights = jnp.where(allowed[:, None, :], jnp.exp(scores), 0.0)
            total = lax.optimization_barrier(jnp.sum(weights, axis=-1, keepdims=True))
            total = jnp.where(live_rows[:, None, None], total, 1.0)
            probs = jnp.where(live_rows[:, None, None], weights / total, 0.0).astype(jnp.bfloat16)
            result = jnp.einsum('tgs,sd->tgd', probs.astype(jnp.float32), value_head.astype(jnp.float32))
            return result.astype(jnp.bfloat16)
        head_out = lax.map(per_head, (jnp.transpose(query_group, (1, 0, 2, 3)), jnp.transpose(key_group, (1, 0, 2)), jnp.transpose(value_group, (1, 0, 2))))
        return jnp.transpose(head_out, (1, 0, 2, 3)).reshape(TEXT_G, QH * HD)
    attended = lax.map(per_group, (query_rows, tiles_first, tiles_both, offsets, text_first, text_both))
    return attended.reshape(N_GRP * TEXT_G, QH * HD)

def math_sqrt(number):
    return float(number) ** 0.5
```

```python
import functools

import jax
import jax.numpy as jnp
from jax import lax
from jax.experimental import pallas as pl
from jax.experimental.pallas import tpu as pltpu
from jax.sharding import PartitionSpec as P

KVH = 8
HD = 128
MAXT = 4
REQ_G = 2
CAP = REQ_G * MAXT

epsilon = 1e-05
MESH = pl.DeviceIdType.MESH
VMEM_BYTES = 60 * 1024 * 1024
LOG2E = 1.4426950408889634
V_SCALE = 2.0**-14
F32 = jnp.float32
BF16 = jnp.bfloat16


def fused_kernel(
    sizes,
    x_hbm,
    taps_hbm,
    gain_ref,
    bias_ref,
    wup_hbm,
    bup_ref,
    wdn_hbm,
    bdn_ref,
    wko_hbm,
    wkt_hbm,
    kgain_ref,
    qgain_ref,
    q_hbm,
    tiles_ref,
    owner_ref,
    text_ref,
    out_hbm,
    xg,
    normed,
    hidden,
    tapst,
    taps,
    wup,
    wdn,
    wko,
    wkt,
    kvt,
    encoded,
    m_send,
    m_r1,
    m_s2,
    m_r2,
    k_send,
    k_r1,
    k_s2,
    k_r2,
    kwin,
    vwin,
    qbuf,
    obuf,
    *rest,
):
    tp_n, grp_n, nch, chan, kv_heads = sizes
    kvs, sems = rest[:kv_heads], rest[kv_heads:]
    (
        w_sem,
        x_ssem,
        x_rsem,
        xp_ssem,
        xp_rsem,
        l1_ssem,
        l1_rsem,
        l2_ssem,
        l2_rsem,
        z_ssem,
        z_rsem,
        o_sem,
    ) = sems
    places, depth, tile = xg.shape
    total_tiles = places * grp_n
    per = places // nch
    rc = per * tile
    chips = tp_n // 2
    order = sorted(range(places), key=lambda k: (abs(2 * k - (places - 1)), k))
    tp_i = lax.axis_index("tp")
    grp_i = lax.axis_index("grp")
    core = lax.rem(tp_i, 2)
    chip = tp_i // 2
    other = 1 - core
    partner = {"tp": chip * 2 + other}

    def peer(dy):
        return lax.rem(chip + dy, chips)

    def peer_id(dy):
        return {"tp": peer(dy) * 2 + core}

    def share(slot):
        return pl.ds(pl.multiple_of(slot * chan, 16), chan)

    names = ["taps", "wkt", "wup", "wdn", "q", "wko"]
    sources = [
        (taps_hbm, tapst),
        (wkt_hbm, wkt),
        (wup_hbm, wup),
        (wdn_hbm, wdn),
        (q_hbm, qbuf),
        (wko_hbm, wko),
    ]
    loads = {
        name: pltpu.make_async_copy(src, dst, w_sem.at[i])
        for i, (name, (src, dst)) in enumerate(zip(names, sources))
    }
    own_x = [
        pltpu.make_async_copy(x_hbm.at[order[pos]], xg.at[pos, share(tp_i)], w_sem.at[6 + pos])
        for pos in range(places)
    ]
    for c in own_x:
        c.start()
    for name in names:
        loads[name].start()

    barrier = pltpu.get_barrier_semaphore()
    pl.semaphore_signal(barrier, inc=1, device_id=partner, device_id_type=MESH)
    for dy in range(1, chips):
        pl.semaphore_signal(barrier, inc=1, device_id=peer_id(dy), device_id_type=MESH)

    @pl.when(grp_i > 0)
    def _():
        pl.semaphore_signal(barrier, inc=1, device_id={"grp": grp_i - 1}, device_id_type=MESH)

    @pl.when(grp_i < grp_n - 1)
    def _():
        pl.semaphore_signal(barrier, inc=1, device_id={"grp": grp_i + 1}, device_id_type=MESH)

    neighbours = jnp.where(grp_i > 0, 1, 0) + jnp.where(grp_i < grp_n - 1, 1, 0)
    pl.semaphore_wait(barrier, chips + neighbours)

    def rows(ch):
        return pl.ds(ch * rc, rc)

    def x_copy(pos, dy):
        return pltpu.make_async_remote_copy(
            src_ref=x_hbm.at[order[pos]],
            dst_ref=xg.at[pos, share(tp_i)],
            send_sem=x_ssem.at[pos, dy],
            recv_sem=x_rsem.at[pos, dy],
            device_id=peer_id(dy) if dy else partner,
            device_id_type=MESH,
        )

    def x_pass(pos, dy):
        slot = lax.rem(chip - dy + chips, chips) * 2 + core
        return pltpu.make_async_remote_copy(
            src_ref=xg.at[pos, share(slot)],
            dst_ref=xg.at[pos, share(slot)],
            send_sem=xp_ssem.at[pos, dy],
            recv_sem=xp_rsem.at[pos, dy],
            device_id=partner,
            device_id_type=MESH,
        )

    def x_forward(pos):
        for dy in range(1, chips):
            x_copy(pos, dy).wait_recv()
            x_pass(pos, dy).start()

    for pos in range(places):
        for dy in list(range(1, chips)) + [0]:
            x_copy(pos, dy).start()

    def head_start(t, h):
        return (t * KVH // tp_n + h) * (2 * HD)

    kv_cols = kvt.shape[1]
    step = 2 * HD

    def tap_rows(pos):
        taps[pos * tile : (pos + 1) * tile, :] = tapst[order[pos]].T

    def tap_product(piece, pieces):
        count = kv_cols // step // pieces

        def body(j, carry):
            at = piece * count + j
            block = lax.rem(at * kv_heads, kv_cols // step) + at * kv_heads // (kv_cols // step)
            cols = pl.ds(pl.multiple_of(block * step, step), step)
            kvt[:, cols] = jnp.dot(taps[...], wkt[:, cols], preferred_element_type=F32)
            return carry

        lax.fori_loop(0, count, body, 0)

    units = hidden.shape[1]

    def up(ch):
        for pos in range(ch * per, (ch + 1) * per):
            own_x[pos].wait()
            x_copy(pos, 0).wait_recv()
            for dy in range(1, chips):
                x_pass(pos, dy).wait_recv()
            blocks = [slice(b * HD, (b + 1) * HD) for b in range(depth // HD)]
            total = jnp.zeros((8, tile), F32)
            for b in blocks:
                values = xg[pos, b, :].astype(F32)
                total = total + jnp.sum(values.reshape(HD // 8, 8, tile), axis=0)
            average = jnp.sum(total, axis=0, keepdims=True) / depth
            square = jnp.zeros((8, tile), F32)
            for b in blocks:
                centered = xg[pos, b, :].astype(F32) - average
                square = square + jnp.sum((centered * centered).reshape(HD // 8, 8, tile), axis=0)
            factor = lax.rsqrt(jnp.sum(square, axis=0, keepdims=True) / depth + epsilon)
            inside = slice((pos - ch * per) * tile, (pos - ch * per + 1) * tile)
            for b in blocks:
                scaled = ((xg[pos, b, :].astype(F32) - average) * factor).T
                normed[inside, b] = (
                    scaled * gain_ref[b].reshape(1, HD) + bias_ref[b].reshape(1, HD)
                ).astype(BF16)
        if ch == 0:
            loads["wup"].wait()
        for j in range(0, units, 256):
            cols = slice(j, min(j + 256, units))
            pre = jnp.dot(normed[...], wup[:, cols], preferred_element_type=F32)
            pre = pre + bup_ref[cols].reshape(1, -1)
            hidden[:, cols] = (0.5 * pre * (1.0 + lax.erf(pre * (0.5**0.5)))).astype(BF16)

    def down(ch):
        if ch == 0:
            loads["wdn"].wait()
        terms = jnp.dot(hidden[...], wdn[...], preferred_element_type=F32).astype(BF16).T
        for t in range(tp_n):
            m_send[ch, t % 2, t // 2] = terms[t * chan : (t + 1) * chan, :]

    def buffers(stage):
        which, at = stage
        if which == 0:
            return (b.at[at] for b in (m_send, m_r1, m_s2, m_r2))
        return (b.at[at] for b in (k_send, k_r1, k_s2, k_r2))

    def number(stage):
        which, at = stage
        return at if which == 0 else nch + at

    def l1(stage):
        send, r1, _, _ = buffers(stage)
        return pltpu.make_async_remote_copy(
            src_ref=send.at[other],
            dst_ref=r1,
            send_sem=l1_ssem.at[number(stage)],
            recv_sem=l1_rsem.at[number(stage)],
            device_id=partner,
            device_id_type=MESH,
        )

    def l2(stage, dy):
        _, _, s2, r2 = buffers(stage)
        return pltpu.make_async_remote_copy(
            src_ref=s2.at[dy - 1],
            dst_ref=r2.at[dy - 1],
            send_sem=l2_ssem.at[number(stage), dy - 1],
            recv_sem=l2_rsem.at[number(stage), dy - 1],
            device_id=peer_id(dy),
            device_id_type=MESH,
        )

    def level2(stage):
        send, r1, s2, _ = buffers(stage)
        l1(stage).wait_recv()
        for dy in range(1, chips):
            y = peer(dy)
            s2[dy - 1] = (send[core, y].astype(F32) + r1[y].astype(F32)).astype(BF16)
            l2(stage, dy).start()

    def summed(stage):
        send, r1, _, r2 = buffers(stage)
        total = send[core, chip].astype(F32) + r1[chip].astype(F32)
        for dy in range(1, chips):
            l2(stage, dy).wait_recv()
            total = total + r2[dy - 1].astype(F32)
        return total

    def encode(ch):
        total = summed((0, ch))
        for p in range(per):
            pos = ch * per + p
            here = total[:, p * tile : (p + 1) * tile] + xg[pos, share(tp_i), :].astype(F32)
            encoded[pos * tile : (pos + 1) * tile, :] = (
                here.T + bdn_ref[...].reshape(1, chan)
            ).astype(BF16)

    def project(h, ch):
        if h == 0 and ch == 0:
            loads["wko"].wait()
        for t in range(tp_n):
            cols = slice(head_start(t, h), head_start(t, h) + step)
            k_send[h * nch + ch, t % 2, t // 2] = (
                jnp.dot(encoded[rows(ch), :], wko[:, cols], preferred_element_type=F32)
                + kvt[rows(ch), cols]
            ).astype(BF16)
        l1((1, h * nch + ch)).start()

    def finish(h, ch):
        total = summed((1, h * nch + ch))
        key = total[:, :HD]
        square = jnp.mean(key * key, axis=-1, keepdims=True)
        key = (key * lax.rsqrt(square + epsilon) * kgain_ref[...].reshape(1, HD)).astype(BF16)
        value = total[:, HD:].astype(BF16)
        for p in range(per):
            pos = ch * per + p
            at = order[pos] * grp_n + grp_i
            kvs[h][at, :, :HD] = key[p * tile : (p + 1) * tile]
            kvs[h][at, :, HD:] = value[p * tile : (p + 1) * tile]
            z_start(h, pos, 0)

    def reaches_up(index, q):
        return (index >= REQ_G * q) & (index >= total_tiles - CAP * (grp_n - q))

    def reaches_down(index, q):
        return (index < total_tiles - REQ_G * (grp_n - 1 - q)) & (index < CAP * (q + 1))

    def z_copy(h, pos, way, k):
        block = jnp.clip(grp_i - k if way == 0 else grp_i + k, 0, grp_n - 1)
        at = order[pos] * grp_n + block
        return pltpu.make_async_remote_copy(
            src_ref=kvs[h].at[at],
            dst_ref=kvs[h].at[at],
            send_sem=z_ssem.at[h, way, pos, k],
            recv_sem=z_rsem.at[h, way, pos, k],
            device_id={"grp": grp_i + 1 if way == 0 else grp_i - 1},
            device_id_type=MESH,
        )

    def z_sends(pos, way, k):
        base = order[pos] * grp_n
        if way == 0:
            return (grp_i - k >= 0) & (grp_i < grp_n - 1) & reaches_up(base + grp_i - k, grp_i + 1)
        return (grp_i + k <= grp_n - 1) & (grp_i > 0) & reaches_down(base + grp_i + k, grp_i - 1)

    def z_gets(pos, way, k):
        base = order[pos] * grp_n
        if way == 0:
            return (grp_i - k - 1 >= 0) & reaches_up(base + grp_i - k - 1, grp_i)
        return (grp_i + k + 1 <= grp_n - 1) & reaches_down(base + grp_i + k + 1, grp_i)

    def z_start(h, pos, k):
        for way in range(2):

            @pl.when(z_sends(pos, way, k))
            def _(way=way):
                z_copy(h, pos, way, k).start()

    def z_hop(h, pos, k):
        for way in range(2):

            @pl.when(z_gets(pos, way, k))
            def _(way=way):
                z_copy(h, pos, way, k).wait_recv()

        if k + 1 < grp_n - 1:
            z_start(h, pos, k + 1)

    text_rows = qbuf.shape[0]
    q_heads = qbuf.shape[1] // HD
    per_kv = q_heads // kv_heads
    half = text_rows // REQ_G
    window = min(MAXT, total_tiles)

    offset = jnp.int32(0)
    tiles = [jnp.int32(0), jnp.int32(0)]
    texts = [jnp.int32(0), jnp.int32(0)]
    seen = jnp.int32(0)
    for r in range(owner_ref.shape[0]):
        own = owner_ref[r] == grp_i
        offset = offset + jnp.where(owner_ref[r] < grp_i, tiles_ref[r], 0)
        for i in range(REQ_G):
            here = own & (seen == i)
            tiles[i] = jnp.where(here, tiles_ref[r], tiles[i])
            texts[i] = jnp.where(here, text_ref[r], texts[i])
        seen = seen + own.astype(jnp.int32)

    def head_cols(qh):
        return pl.ds(pl.multiple_of(qh * HD, HD), HD)

    def norm_queries(low, high):
        def body(qh, carry):
            query = qbuf[:, head_cols(qh)].astype(F32)
            square = jnp.mean(query * query, axis=-1, keepdims=True)
            gain = qgain_ref[...].reshape(1, HD) * (LOG2E / float(HD) ** 0.5)
            qbuf[:, head_cols(qh)] = (query * lax.rsqrt(square + epsilon) * gain).astype(BF16)
            return carry

        lax.fori_loop(low, high, body, 0)

    def windows(h):
        for i in range(REQ_G):
            low = offset if i == 0 else offset + tiles[0]
            start = jnp.minimum(low, total_tiles - window)
            here = kvs[h][pl.ds(start, window)].reshape(window * tile, 2 * HD)
            row = lax.broadcasted_iota(jnp.int32, (window * tile, HD), 0) + start * tile
            valid = (row >= low * tile) & (row < (low + tiles[i]) * tile)
            kwin[i] = jnp.where(valid, here[:, :HD].astype(F32), 0.0).astype(BF16)
            vwin[i, :, :HD] = jnp.where(valid, here[:, HD:].astype(F32) * V_SCALE, 0.0).astype(BF16)
            vwin[i, :, HD:] = jnp.where(valid, V_SCALE, 0.0).astype(BF16)

    def scores(query, i):
        return lax.dot_general(
            query, kwin[i], (((1,), (1,)), ((), ())), preferred_element_type=F32
        )

    def attend(low, high):
        row = lax.broadcasted_iota(jnp.int32, (half, 1), 0)
        first = row < texts[0]
        live = row + half < texts[0] + texts[1]

        def body(qh, carry):
            query = qbuf[:half, head_cols(qh)]
            both = jnp.where(first, scores(query, 0), scores(query, 1))
            weights = jnp.exp2(both).astype(BF16)
            result = jnp.where(
                first,
                jnp.dot(weights, vwin[0], preferred_element_type=F32),
                jnp.dot(weights, vwin[1], preferred_element_type=F32),
            )
            top = row < texts[0] + texts[1]
            obuf[:half, head_cols(qh)] = jnp.where(top, result[:, :HD] / result[:, HD:], 0.0).astype(
                BF16
            )
            query = qbuf[half:, head_cols(qh)]
            weights = jnp.exp2(scores(query, 1)).astype(BF16)
            result = jnp.dot(weights, vwin[1], preferred_element_type=F32)
            obuf[half:, head_cols(qh)] = jnp.where(
                live, result[:, :HD] / result[:, HD:], 0.0
            ).astype(BF16)
            return carry

        lax.fori_loop(low, high, body, 0)

    def out_copy(h):
        cols = pl.ds(h * per_kv * HD, per_kv * HD)
        return pltpu.make_async_copy(obuf.at[:, cols], out_hbm.at[:, cols], o_sem.at[h])

    loads["taps"].wait()
    for pos in range(places):
        tap_rows(pos)
    loads["wkt"].wait()
    pieces = 4
    done = 0
    for pos in range(places):
        if pos % 2 == 0:
            tap_product(done, pieces)
            done += 1
        x_forward(pos)

    up(0)
    down(0)
    l1((0, 0)).start()
    for ch in range(1, nch):
        up(ch)
        level2((0, ch - 1))
        down(ch)
        l1((0, ch)).start()
    if done < pieces:
        tap_product(done, pieces)
        done += 1
    level2((0, nch - 1))
    while done < pieces:
        tap_product(done, pieces)
        done += 1
    loads["q"].wait()
    norm_queries(0, q_heads)

    stages = [(h, ch) for h in range(kv_heads) for ch in range(nch)]
    for j, (h, ch) in enumerate(stages):
        if h == 0:
            encode(ch)
        project(h, ch)
        if j > 0:
            level2((1, j - 1))
    level2((1, len(stages) - 1))

    last = grp_n - 2

    def chunk(ch):
        return range(ch * per, (ch + 1) * per)

    for h in range(kv_heads):
        if h == 0:
            for ch in range(nch):
                finish(0, ch)
            for k in range(last):
                for pos in range(places):
                    z_hop(0, pos, k)
                for ch in range(nch):
                    if kv_heads > 1 and k == ch:
                        finish(1, ch)
        if h == 0 and kv_heads > 1:
            for ch in range(last, nch):
                finish(1, ch)
        for pos in range(places):
            z_hop(h, pos, last)
        windows(h)
        base = h * per_kv
        if h + 1 < kv_heads:
            parts = last + 1
            edges = [per_kv * p // parts for p in range(parts + 1)]
            for k in range(parts):
                attend(base + edges[k], base + edges[k + 1])
                if k < last:
                    for pos in range(places):
                        z_hop(h + 1, pos, k)
        else:
            attend(base, base + per_kv)
        out_copy(h).start()

    for pos in range(places):
        for dy in range(chips):
            x_copy(pos, dy).wait_send()
        for dy in range(1, chips):
            x_pass(pos, dy).wait_send()
    for stage in [(0, ch) for ch in range(nch)] + [(1, j) for j in range(len(stages))]:
        l1(stage).wait_send()
        for dy in range(1, chips):
            l2(stage, dy).wait_send()
    for h in range(kv_heads):
        for pos in range(places):
            for k in range(grp_n - 1):
                for way in range(2):

                    @pl.when(z_sends(pos, way, k))
                    def _(h=h, pos=pos, way=way, k=k):
                        z_copy(h, pos, way, k).wait_send()

    for h in range(kv_heads):
        out_copy(h).wait()


def local(
    x_in,
    taps,
    ln_gain,
    ln_bias,
    w_up,
    b_up,
    w_down,
    b_down,
    kv_w_out,
    kv_w_taps,
    k_gain,
    q_gain,
    queries,
    tiles_per_request,
    owner,
    text_per_request,
):
    grp_n = lax.axis_size("grp")
    tp_n = lax.axis_size("tp")
    chips = tp_n // 2
    places, _, tile, chan = x_in.shape
    n = places * tile
    nch = 2 if places % 2 == 0 else 1
    rc = n // nch
    depth, units = w_up.shape
    tap_share, kv_cols = kv_w_taps.shape
    kv_heads = max(1, KVH // tp_n)
    width = 2 * HD
    stages = kv_heads * nch
    text_rows, query_width = queries.shape
    window = min(MAXT, places * grp_n) * tile
    any_spec = pl.BlockSpec(memory_space=pl.ANY)
    vmem_spec = pl.BlockSpec(memory_space=pltpu.VMEM)
    smem_spec = pl.BlockSpec(memory_space=pltpu.SMEM)
    dma = pltpu.SemaphoreType.DMA
    return pl.pallas_call(
        functools.partial(fused_kernel, (tp_n, grp_n, nch, chan, kv_heads)),
        name="fused",
        out_shape=jax.ShapeDtypeStruct(queries.shape, BF16),
        in_specs=[
            any_spec,
            any_spec,
            vmem_spec,
            vmem_spec,
            any_spec,
            vmem_spec,
            any_spec,
            vmem_spec,
            any_spec,
            any_spec,
            vmem_spec,
            vmem_spec,
            any_spec,
            smem_spec,
            smem_spec,
            smem_spec,
        ],
        out_specs=any_spec,
        scratch_shapes=[
            pltpu.VMEM((places, depth, tile), BF16),
            pltpu.VMEM((rc, depth), BF16),
            pltpu.VMEM((rc, units), BF16),
            pltpu.VMEM((places, tap_share, tile), BF16),
            pltpu.VMEM((n, tap_share), BF16),
            pltpu.VMEM(w_up.shape, BF16),
            pltpu.VMEM(w_down.shape, BF16),
            pltpu.VMEM(kv_w_out.shape, BF16),
            pltpu.VMEM(kv_w_taps.shape, BF16),
            pltpu.VMEM((n, kv_cols), F32),
            pltpu.VMEM((n, chan), BF16),
            pltpu.VMEM((nch, 2, chips, chan, rc), BF16),
            pltpu.VMEM((nch, chips, chan, rc), BF16),
            pltpu.VMEM((nch, chips - 1, chan, rc), BF16),
            pltpu.VMEM((nch, chips - 1, chan, rc), BF16),
            pltpu.VMEM((stages, 2, chips, rc, width), BF16),
            pltpu.VMEM((stages, chips, rc, width), BF16),
            pltpu.VMEM((stages, chips - 1, rc, width), BF16),
            pltpu.VMEM((stages, chips - 1, rc, width), BF16),
            pltpu.VMEM((REQ_G, window, HD), BF16),
            pltpu.VMEM((REQ_G, window, 2 * HD), BF16),
            pltpu.VMEM((text_rows, query_width), BF16),
            pltpu.VMEM((text_rows, query_width), BF16),
        ]
        + [pltpu.VMEM((places * grp_n, tile, width), BF16) for _ in range(kv_heads)]
        + [
            dma((6 + places,)),
            dma((places, chips)),
            dma((places, chips)),
            dma((places, chips)),
            dma((places, chips)),
            dma((nch + stages,)),
            dma((nch + stages,)),
            dma((nch + stages, chips - 1)),
            dma((nch + stages, chips - 1)),
            dma((kv_heads, 2, places, grp_n - 1)),
            dma((kv_heads, 2, places, grp_n - 1)),
            dma((kv_heads,)),
        ],
        compiler_params=pltpu.CompilerParams(
            collective_id=0, has_side_effects=True, vmem_limit_bytes=VMEM_BYTES
        ),
    )(
        jnp.transpose(x_in, (0, 1, 3, 2)).reshape(places, chan, tile),
        jnp.transpose(taps, (0, 1, 3, 2)).reshape(places, tap_share, tile),
        ln_gain,
        ln_bias,
        w_up,
        b_up,
        w_down,
        b_down,
        kv_w_out,
        kv_w_taps,
        k_gain,
        q_gain,
        queries,
        tiles_per_request,
        owner,
        text_per_request,
    )


def solution(mesh):
    in_specs = (
        P(None, ("rep", "grp"), None, "tp"),
        P(None, ("rep", "grp"), None, "tp"),
        P(),
        P(),
        P(None, "tp"),
        P("tp"),
        P("tp", None),
        P("tp"),
        P("tp", None),
        P("tp", None),
        P(),
        P(),
        P(("rep", "grp"), "tp"),
        P("rep"),
        P("rep"),
        P("rep"),
    )
    out_specs = P(("rep", "grp"), "tp")
    return jax.shard_map(local, mesh=mesh, in_specs=in_specs, out_specs=out_specs, check_vma=False)
```

```python
import functools

import jax
import jax.numpy as jnp
from jax import lax
from jax.experimental import pallas as pl
from jax.experimental.pallas import tpu as pltpu
from jax.sharding import PartitionSpec as P

KVH = 8
HD = 128
MAXT = 4
REQ_G = 2
CAP = REQ_G * MAXT

epsilon = 1e-05
MESH = pl.DeviceIdType.MESH
VMEM_BYTES = 60 * 1024 * 1024
LOG2E = 1.4426950408889634
V_SCALE = 2.0**-14
F32 = jnp.float32
BF16 = jnp.bfloat16


def fused_kernel(
    sizes,
    x_hbm,
    taps_hbm,
    gain_ref,
    bias_ref,
    wup_hbm,
    bup_ref,
    wdn_hbm,
    bdn_ref,
    wko_hbm,
    wkt_hbm,
    kgain_ref,
    qgain_ref,
    q_hbm,
    tiles_ref,
    owner_ref,
    text_ref,
    out_ref,
    xg,
    normed,
    hidden,
    tapst,
    taps,
    wup,
    wdn,
    wko,
    wkt,
    kvt,
    encoded,
    m_send,
    m_r1,
    m_s2,
    m_r2,
    k_send,
    k_r1,
    k_s2,
    k_r2,
    kwin,
    vwin,
    qbuf,
    qnorm,
    qrows,
    orows,
    *rest,
):
    tp_n, grp_n, nch, chan, kv_heads = sizes
    kvs, sems = rest[:kv_heads], rest[kv_heads:]
    (
        w_sem,
        x_ssem,
        x_rsem,
        xp_ssem,
        xp_rsem,
        l1_ssem,
        l1_rsem,
        l2_ssem,
        l2_rsem,
        z_ssem,
        z_rsem,
    ) = sems
    places, depth, tile = xg.shape
    total_tiles = places * grp_n
    per = places // nch
    rc = per * tile
    chips = tp_n // 2
    order = sorted(range(places), key=lambda k: (abs(2 * k - (places - 1)), k))
    tp_i = lax.axis_index("tp")
    grp_i = lax.axis_index("grp")
    core = lax.rem(tp_i, 2)
    chip = tp_i // 2
    other = 1 - core
    partner = {"tp": chip * 2 + other}

    def peer(dy):
        return lax.rem(chip + dy, chips)

    def peer_id(dy):
        return {"tp": peer(dy) * 2 + core}

    def share(slot):
        return pl.ds(pl.multiple_of(slot * chan, 16), chan)

    names = ["taps", "wkt", "wup", "wdn", "q", "wko"]
    sources = [
        (taps_hbm, tapst),
        (wkt_hbm, wkt),
        (wup_hbm, wup),
        (wdn_hbm, wdn),
        (q_hbm, qbuf),
        (wko_hbm, wko),
    ]
    loads = {
        name: pltpu.make_async_copy(src, dst, w_sem.at[i])
        for i, (name, (src, dst)) in enumerate(zip(names, sources))
    }
    own_x = [
        pltpu.make_async_copy(x_hbm.at[order[pos]], xg.at[pos, share(tp_i)], w_sem.at[6 + pos])
        for pos in range(places)
    ]
    for c in own_x:
        c.start()
    for name in names:
        loads[name].start()

    barrier = pltpu.get_barrier_semaphore()
    pl.semaphore_signal(barrier, inc=1, device_id=partner, device_id_type=MESH)
    for dy in range(1, chips):
        pl.semaphore_signal(barrier, inc=1, device_id=peer_id(dy), device_id_type=MESH)

    @pl.when(grp_i > 0)
    def _():
        pl.semaphore_signal(barrier, inc=1, device_id={"grp": grp_i - 1}, device_id_type=MESH)

    @pl.when(grp_i < grp_n - 1)
    def _():
        pl.semaphore_signal(barrier, inc=1, device_id={"grp": grp_i + 1}, device_id_type=MESH)

    neighbours = jnp.where(grp_i > 0, 1, 0) + jnp.where(grp_i < grp_n - 1, 1, 0)
    pl.semaphore_wait(barrier, chips + neighbours)

    def rows(ch):
        return pl.ds(ch * rc, rc)

    def x_copy(pos, dy):
        return pltpu.make_async_remote_copy(
            src_ref=x_hbm.at[order[pos]],
            dst_ref=xg.at[pos, share(tp_i)],
            send_sem=x_ssem.at[pos, dy],
            recv_sem=x_rsem.at[pos, dy],
            device_id=peer_id(dy) if dy else partner,
            device_id_type=MESH,
        )

    def x_pass(pos, dy):
        slot = lax.rem(chip - dy + chips, chips) * 2 + core
        return pltpu.make_async_remote_copy(
            src_ref=xg.at[pos, share(slot)],
            dst_ref=xg.at[pos, share(slot)],
            send_sem=xp_ssem.at[pos, dy],
            recv_sem=xp_rsem.at[pos, dy],
            device_id=partner,
            device_id_type=MESH,
        )

    def x_forward(pos):
        for dy in range(1, chips):
            x_copy(pos, dy).wait_recv()
            x_pass(pos, dy).start()

    for pos in range(places):
        for dy in list(range(1, chips)) + [0]:
            x_copy(pos, dy).start()

    kv_cols = kvt.shape[1]
    step = 2 * HD

    def tap_rows(pos):
        taps[pos * tile : (pos + 1) * tile, :] = tapst[order[pos]].T

    tap_blocks = kv_cols // step

    def tap_product(low, high):
        def body(at, carry):
            block = lax.rem(at * kv_heads, tap_blocks) + at * kv_heads // tap_blocks
            cols = pl.ds(pl.multiple_of(block * step, step), step)
            kvt[:, cols] = jnp.dot(taps[...], wkt[:, cols], preferred_element_type=F32)
            return carry

        lax.fori_loop(low, high, body, 0)

    units = hidden.shape[1]

    def layer_norm(ch):
        for pos in range(ch * per, (ch + 1) * per):
            own_x[pos].wait()
            x_copy(pos, 0).wait_recv()
            for dy in range(1, chips):
                x_pass(pos, dy).wait_recv()
            blocks = [slice(b * HD, (b + 1) * HD) for b in range(depth // HD)]
            total = jnp.zeros((8, tile), F32)
            for b in blocks:
                values = xg[pos, b, :].astype(F32)
                total = total + jnp.sum(values.reshape(HD // 8, 8, tile), axis=0)
            average = jnp.sum(total, axis=0, keepdims=True) / depth
            square = jnp.zeros((8, tile), F32)
            for b in blocks:
                centered = xg[pos, b, :].astype(F32) - average
                square = square + jnp.sum((centered * centered).reshape(HD // 8, 8, tile), axis=0)
            factor = lax.rsqrt(jnp.sum(square, axis=0, keepdims=True) / depth + epsilon)
            inside = slice((pos - ch * per) * tile, (pos - ch * per + 1) * tile)
            for b in blocks:
                scaled = ((xg[pos, b, :].astype(F32) - average) * factor).T
                normed[inside, b] = (
                    scaled * gain_ref[b].reshape(1, HD) + bias_ref[b].reshape(1, HD)
                ).astype(BF16)

    def up(ch, low, high):
        if ch == 0 and low == 0:
            loads["wup"].wait()
        for j in range(low, high, 256):
            cols = slice(j, min(j + 256, high))
            pre = jnp.dot(normed[...], wup[:, cols], preferred_element_type=F32)
            pre = pre + bup_ref[cols].reshape(1, -1)
            hidden[:, cols] = (0.5 * pre * (1.0 + lax.erf(pre * (0.5**0.5)))).astype(BF16)

    def down(ch):
        if ch == 0:
            loads["wdn"].wait()
        terms = jnp.dot(hidden[...], wdn[...], preferred_element_type=F32).astype(BF16).T
        for t in range(tp_n):
            m_send[ch, t % 2, t // 2] = terms[t * chan : (t + 1) * chan, :]
        start_l1((0, ch))

    def buffers(stage):
        which, at = stage
        if which == 0:
            return (b.at[at] for b in (m_send, m_r1, m_s2, m_r2))
        return (b.at[at] for b in (k_send, k_r1, k_s2, k_r2))

    def number(stage):
        which, at = stage
        return at if which == 0 else nch + at

    def l1(stage, dy):
        send, r1, _, _ = buffers(stage)
        y = peer(dy)
        return pltpu.make_async_remote_copy(
            src_ref=send.at[other, y],
            dst_ref=r1.at[y],
            send_sem=l1_ssem.at[number(stage), dy],
            recv_sem=l1_rsem.at[number(stage), dy],
            device_id=partner,
            device_id_type=MESH,
        )

    def start_l1(stage):
        for dy in list(range(1, chips)) + [0]:
            l1(stage, dy).start()

    def l2(stage, dy):
        _, _, s2, r2 = buffers(stage)
        return pltpu.make_async_remote_copy(
            src_ref=s2.at[dy - 1],
            dst_ref=r2.at[dy - 1],
            send_sem=l2_ssem.at[number(stage), dy - 1],
            recv_sem=l2_rsem.at[number(stage), dy - 1],
            device_id=peer_id(dy),
            device_id_type=MESH,
        )

    def level2(stage):
        send, r1, s2, _ = buffers(stage)
        for dy in range(1, chips):
            y = peer(dy)
            l1(stage, dy).wait_recv()
            s2[dy - 1] = (send[core, y].astype(F32) + r1[y].astype(F32)).astype(BF16)
            l2(stage, dy).start()

    def summed(stage):
        send, r1, _, r2 = buffers(stage)
        l1(stage, 0).wait_recv()
        total = send[core, chip].astype(F32) + r1[chip].astype(F32)
        for dy in range(1, chips):
            l2(stage, dy).wait_recv()
            total = total + r2[dy - 1].astype(F32)
        return total

    def encode(ch):
        total = summed((0, ch))
        for p in range(per):
            pos = ch * per + p
            here = total[:, p * tile : (p + 1) * tile] + xg[pos, share(tp_i), :].astype(F32)
            encoded[pos * tile : (pos + 1) * tile, :] = (
                here.T + bdn_ref[...].reshape(1, chan)
            ).astype(BF16)

    def project(h, ch):
        if h == 0 and ch == 0:
            loads["wko"].wait()
        at = h * nch + ch
        for dy in list(range(1, chips)) + [0]:
            y = peer(dy)
            for side in (other, core):
                start = (lax.div((y * 2 + side) * KVH, tp_n) + h) * step
                cols = pl.ds(pl.multiple_of(start, step), step)
                k_send[at, side, y] = (
                    jnp.dot(encoded[rows(ch), :], wko[:, cols], preferred_element_type=F32)
                    + kvt[rows(ch), cols]
                ).astype(BF16)
                if side is other:
                    l1((1, at), dy).start()

    def finish(h, ch):
        total = summed((1, h * nch + ch))
        key = total[:, :HD]
        square = jnp.mean(key * key, axis=-1, keepdims=True)
        key = (key * lax.rsqrt(square + epsilon) * kgain_ref[...].reshape(1, HD)).astype(BF16)
        value = total[:, HD:].astype(BF16)
        for p in range(per):
            pos = ch * per + p
            at = order[pos] * grp_n + grp_i
            kvs[h][at, :, :HD] = key[p * tile : (p + 1) * tile]
            kvs[h][at, :, HD:] = value[p * tile : (p + 1) * tile]
            z_start(h, pos, 0)

    def reaches_up(index, q):
        return (index >= REQ_G * q) & (index >= total_tiles - CAP * (grp_n - q))

    def reaches_down(index, q):
        return (index < total_tiles - REQ_G * (grp_n - 1 - q)) & (index < CAP * (q + 1))

    def z_copy(h, pos, way, k):
        block = jnp.clip(grp_i - k if way == 0 else grp_i + k, 0, grp_n - 1)
        at = order[pos] * grp_n + block
        return pltpu.make_async_remote_copy(
            src_ref=kvs[h].at[at],
            dst_ref=kvs[h].at[at],
            send_sem=z_ssem.at[h, way, pos, k],
            recv_sem=z_rsem.at[h, way, pos, k],
            device_id={"grp": grp_i + 1 if way == 0 else grp_i - 1},
            device_id_type=MESH,
        )

    def z_sends(pos, way, k):
        base = order[pos] * grp_n
        if way == 0:
            return (grp_i - k >= 0) & (grp_i < grp_n - 1) & reaches_up(base + grp_i - k, grp_i + 1)
        return (grp_i + k <= grp_n - 1) & (grp_i > 0) & reaches_down(base + grp_i + k, grp_i - 1)

    def z_gets(pos, way, k):
        base = order[pos] * grp_n
        if way == 0:
            return (grp_i - k - 1 >= 0) & reaches_up(base + grp_i - k - 1, grp_i)
        return (grp_i + k + 1 <= grp_n - 1) & reaches_down(base + grp_i + k + 1, grp_i)

    def z_start(h, pos, k):
        for way in range(2):

            @pl.when(z_sends(pos, way, k))
            def _(way=way):
                z_copy(h, pos, way, k).start()

    def z_hop(h, pos, k):
        for way in range(2):

            @pl.when(z_gets(pos, way, k))
            def _(way=way):
                z_copy(h, pos, way, k).wait_recv()

        if k + 1 < grp_n - 1:
            z_start(h, pos, k + 1)

    text_rows = qbuf.shape[0]
    q_heads = qbuf.shape[1] // HD
    per_kv = q_heads // kv_heads
    half = text_rows // REQ_G
    window = min(MAXT, total_tiles)

    offset = jnp.int32(0)
    tiles = [jnp.int32(0), jnp.int32(0)]
    texts = [jnp.int32(0), jnp.int32(0)]
    seen = jnp.int32(0)
    for r in range(owner_ref.shape[0]):
        own = owner_ref[r] == grp_i
        offset = offset + jnp.where(owner_ref[r] < grp_i, tiles_ref[r], 0)
        for i in range(REQ_G):
            here = own & (seen == i)
            tiles[i] = jnp.where(here, tiles_ref[r], tiles[i])
            texts[i] = jnp.where(here, text_ref[r], texts[i])
        seen = seen + own.astype(jnp.int32)

    def head_cols(qh):
        return pl.ds(pl.multiple_of(qh * HD, HD), HD)

    def norm_queries(low, high):
        def body(qh, carry):
            query = qbuf[:, head_cols(qh)].astype(F32)
            square = jnp.mean(query * query, axis=-1, keepdims=True)
            gain = qgain_ref[...].reshape(1, HD) * (LOG2E / float(HD) ** 0.5)
            query = query * lax.rsqrt(square + epsilon) * gain
            qrows[...] = query
            qnorm[0, :, head_cols(qh)] = query[:half].astype(BF16)
            qnorm[1, :, head_cols(qh)] = qrows[pl.ds(texts[0], half), :].astype(BF16)
            return carry

        lax.fori_loop(low, high, body, 0)

    def windows(h):
        for i in range(REQ_G):
            low = offset if i == 0 else offset + tiles[0]
            start = jnp.minimum(low, total_tiles - window)
            here = kvs[h][pl.ds(start, window)].reshape(window * tile, 2 * HD)
            row = lax.broadcasted_iota(jnp.int32, (window * tile, HD), 0) + start * tile
            valid = (row >= low * tile) & (row < (low + tiles[i]) * tile)
            kwin[i] = jnp.where(valid, here[:, :HD].astype(F32), 0.0).astype(BF16)
            vwin[i, :, :HD] = jnp.where(valid, here[:, HD:].astype(F32) * V_SCALE, 0.0).astype(BF16)
            vwin[i, :, HD:] = jnp.where(valid, V_SCALE, 0.0).astype(BF16)

    def attend(low, high):
        row = lax.broadcasted_iota(jnp.int32, (half, 1), 0)
        both = texts[0] + texts[1]
        first = row < texts[0]
        top, bottom = row < both, row + half < both

        def request(qh, i):
            scores = lax.dot_general(
                qnorm[i, :, head_cols(qh)],
                kwin[i],
                (((1,), (1,)), ((), ())),
                preferred_element_type=F32,
            )
            weights = jnp.exp2(scores).astype(BF16)
            result = jnp.dot(weights, vwin[i], preferred_element_type=F32)
            return result[:, :HD] / result[:, HD:]

        def body(pair, carry):
            for slot in range(2):
                qh = pair * 2 + slot
                orows[slot, half : 2 * half] = request(qh, 1)
                moved = orows[slot, pl.ds(half - texts[0], text_rows)]
                mine = request(qh, 0)
                out_ref[:half, head_cols(qh)] = jnp.where(
                    first, mine, jnp.where(top, moved[:half], 0.0)
                ).astype(BF16)
                out_ref[half:, head_cols(qh)] = jnp.where(bottom, moved[half:], 0.0).astype(BF16)
            return carry

        lax.fori_loop(low, high, body, 0)

    loads["taps"].wait()
    for pos in range(places):
        tap_rows(pos)
    loads["wkt"].wait()

    def part(k, of):
        return tap_blocks * k // of

    tap_product(0, part(4, 8))
    for pos in range(per):
        x_forward(pos)
        tap_product(part(4 + 2 * pos // per, 8), part(4 + 2 * (pos + 1) // per, 8))
    layer_norm(0)
    up(0, 0, units)
    split = units * 3 // 5 // 256 * 256
    for ch in range(1, nch):
        x_forward(ch * per)
        down(ch - 1)
        for pos in range(ch * per + 1, (ch + 1) * per):
            x_forward(pos)
        layer_norm(ch)
        up(ch, 0, split)
        level2((0, ch - 1))
        up(ch, split, units)
    down(nch - 1)
    tap_product(part(6, 8), part(7, 8))
    level2((0, nch - 1))
    tap_product(part(7, 8), tap_blocks)
    loads["q"].wait()
    norm_queries(0, per_kv)

    stages = [(h, ch) for h in range(kv_heads) for ch in range(nch)]
    sent = 0
    for ch in range(nch):
        encode(ch)
        for h in range(kv_heads):
            project(h, ch)
        if ch < nch - 1:
            level2((1, ch))
            sent += 1
    for j in range(sent, len(stages)):
        level2((1, j))
    norm_queries(per_kv, q_heads)

    last = grp_n - 2

    def chunk(ch):
        return range(ch * per, (ch + 1) * per)

    for h in range(kv_heads):
        if h == 0:
            for ch in range(nch):
                finish(0, ch)
            for k in range(last):
                for pos in range(places):
                    z_hop(0, pos, k)
                for ch in range(nch):
                    if kv_heads > 1 and k == ch:
                        finish(1, ch)
        if h == 0 and kv_heads > 1:
            for ch in range(last, nch):
                finish(1, ch)
        for pos in range(places):
            z_hop(h, pos, last)
        windows(h)
        base = h * per_kv
        if h + 1 < kv_heads:
            parts = last + 1
            edges = [(base + per_kv * p // parts) // 2 for p in range(parts + 1)]
            for k in range(parts):
                attend(edges[k], edges[k + 1])
                if k < last:
                    for pos in range(places):
                        z_hop(h + 1, pos, k)
        else:
            attend(base // 2, (base + per_kv) // 2)

    for pos in range(places):
        for dy in range(chips):
            x_copy(pos, dy).wait_send()
        for dy in range(1, chips):
            x_pass(pos, dy).wait_send()
    for stage in [(0, ch) for ch in range(nch)] + [(1, j) for j in range(len(stages))]:
        for dy in range(chips):
            l1(stage, dy).wait_send()
        for dy in range(1, chips):
            l2(stage, dy).wait_send()
    for h in range(kv_heads):
        for pos in range(places):
            for k in range(grp_n - 1):
                for way in range(2):

                    @pl.when(z_sends(pos, way, k))
                    def _(h=h, pos=pos, way=way, k=k):
                        z_copy(h, pos, way, k).wait_send()


def local(
    x_in,
    taps,
    ln_gain,
    ln_bias,
    w_up,
    b_up,
    w_down,
    b_down,
    kv_w_out,
    kv_w_taps,
    k_gain,
    q_gain,
    queries,
    tiles_per_request,
    owner,
    text_per_request,
):
    grp_n = lax.axis_size("grp")
    tp_n = lax.axis_size("tp")
    chips = tp_n // 2
    places, _, tile, chan = x_in.shape
    n = places * tile
    nch = 2 if places % 2 == 0 else 1
    rc = n // nch
    depth, units = w_up.shape
    tap_share, kv_cols = kv_w_taps.shape
    kv_heads = max(1, KVH // tp_n)
    width = 2 * HD
    stages = kv_heads * nch
    text_rows, query_width = queries.shape
    half = text_rows // REQ_G
    window = min(MAXT, places * grp_n) * tile
    any_spec = pl.BlockSpec(memory_space=pl.ANY)
    vmem_spec = pl.BlockSpec(memory_space=pltpu.VMEM)
    smem_spec = pl.BlockSpec(memory_space=pltpu.SMEM)
    dma = pltpu.SemaphoreType.DMA
    return pl.pallas_call(
        functools.partial(fused_kernel, (tp_n, grp_n, nch, chan, kv_heads)),
        name="fused",
        out_shape=pltpu.VMEM(queries.shape, BF16),
        in_specs=[
            any_spec,
            any_spec,
            vmem_spec,
            vmem_spec,
            any_spec,
            vmem_spec,
            any_spec,
            vmem_spec,
            any_spec,
            any_spec,
            vmem_spec,
            vmem_spec,
            any_spec,
            smem_spec,
            smem_spec,
            smem_spec,
        ],
        out_specs=vmem_spec,
        scratch_shapes=[
            pltpu.VMEM((places, depth, tile), BF16),
            pltpu.VMEM((rc, depth), BF16),
            pltpu.VMEM((rc, units), BF16),
            pltpu.VMEM((places, tap_share, tile), BF16),
            pltpu.VMEM((n, tap_share), BF16),
            pltpu.VMEM(w_up.shape, BF16),
            pltpu.VMEM(w_down.shape, BF16),
            pltpu.VMEM(kv_w_out.shape, BF16),
            pltpu.VMEM(kv_w_taps.shape, BF16),
            pltpu.VMEM((n, kv_cols), F32),
            pltpu.VMEM((n, chan), BF16),
            pltpu.VMEM((nch, 2, chips, chan, rc), BF16),
            pltpu.VMEM((nch, chips, chan, rc), BF16),
            pltpu.VMEM((nch, chips - 1, chan, rc), BF16),
            pltpu.VMEM((nch, chips - 1, chan, rc), BF16),
            pltpu.VMEM((stages, 2, chips, rc, width), BF16),
            pltpu.VMEM((stages, chips, rc, width), BF16),
            pltpu.VMEM((stages, chips - 1, rc, width), BF16),
            pltpu.VMEM((stages, chips - 1, rc, width), BF16),
            pltpu.VMEM((REQ_G, window, HD), BF16),
            pltpu.VMEM((REQ_G, window, 2 * HD), BF16),
            pltpu.VMEM((text_rows, query_width), BF16),
            pltpu.VMEM((REQ_G, half, query_width), BF16),
            pltpu.VMEM((text_rows, HD), F32),
            pltpu.VMEM((2, half + text_rows, HD), F32),
        ]
        + [pltpu.VMEM((places * grp_n, tile, width), BF16) for _ in range(kv_heads)]
        + [
            dma((6 + places,)),
            dma((places, chips)),
            dma((places, chips)),
            dma((places, chips)),
            dma((places, chips)),
            dma((nch + stages, chips)),
            dma((nch + stages, chips)),
            dma((nch + stages, chips - 1)),
            dma((nch + stages, chips - 1)),
            dma((kv_heads, 2, places, grp_n - 1)),
            dma((kv_heads, 2, places, grp_n - 1)),
        ],
        compiler_params=pltpu.CompilerParams(
            collective_id=0, has_side_effects=True, vmem_limit_bytes=VMEM_BYTES
        ),
    )(
        jnp.transpose(x_in, (0, 1, 3, 2)).reshape(places, chan, tile),
        jnp.transpose(taps, (0, 1, 3, 2)).reshape(places, tap_share, tile),
        ln_gain,
        ln_bias,
        w_up,
        b_up,
        w_down,
        b_down,
        kv_w_out,
        kv_w_taps,
        k_gain,
        q_gain,
        queries,
        tiles_per_request,
        owner,
        text_per_request,
    )


def solution(mesh):
    in_specs = (
        P(None, ("rep", "grp"), None, "tp"),
        P(None, ("rep", "grp"), None, "tp"),
        P(),
        P(),
        P(None, "tp"),
        P("tp"),
        P("tp", None),
        P("tp"),
        P("tp", None),
        P("tp", None),
        P(),
        P(),
        P(("rep", "grp"), "tp"),
        P("rep"),
        P("rep"),
        P("rep"),
    )
    out_specs = P(("rep", "grp"), "tp")
    return jax.shard_map(local, mesh=mesh, in_specs=in_specs, out_specs=out_specs, check_vma=False)
```

```python
import functools

import jax
import jax.numpy as jnp
from jax import lax
from jax.experimental import pallas as pl
from jax.experimental.pallas import tpu as pltpu
from jax.sharding import PartitionSpec as P

KVH = 8
HD = 128
MAXT = 4
REQ_G = 2
CAP = REQ_G * MAXT

epsilon = 1e-05
MESH = pl.DeviceIdType.MESH
VMEM_BYTES = 60 * 1024 * 1024
LOG2E = 1.4426950408889634
V_SCALE = 2.0**-14
F32 = jnp.float32
BF16 = jnp.bfloat16


def fused_kernel(
    sizes,
    x_hbm,
    taps_hbm,
    gain_ref,
    bias_ref,
    wup_hbm,
    bup_ref,
    wdn_hbm,
    bdn_ref,
    wko_hbm,
    wkt_hbm,
    kgain_ref,
    qgain_ref,
    q_hbm,
    tiles_ref,
    owner_ref,
    text_ref,
    out_ref,
    xg,
    normed,
    hidden,
    tapst,
    taps,
    wup,
    wdn,
    wko,
    wkt,
    kvt,
    encoded,
    m_send,
    m_r1,
    m_s2,
    m_r2,
    k_send,
    k_r1,
    k_s2,
    k_r2,
    kwin,
    vwin,
    qbuf,
    qnorm,
    qrows,
    orows,
    obuf,
    *rest,
):
    tp_n, grp_n, nch, chan, kv_heads = sizes
    kvs, sems = rest[:kv_heads], rest[kv_heads:]
    (
        w_sem,
        x_ssem,
        x_rsem,
        xp_ssem,
        xp_rsem,
        l1_ssem,
        l1_rsem,
        l2_ssem,
        l2_rsem,
        z_ssem,
        z_rsem,
        o_sem,
    ) = sems
    places, depth, tile = xg.shape
    total_tiles = places * grp_n
    per = places // nch
    rc = per * tile
    chips = tp_n // 2
    order = sorted(range(places), key=lambda k: (abs(2 * k - (places - 1)), k))
    tp_i = lax.axis_index("tp")
    grp_i = lax.axis_index("grp")
    core = lax.rem(tp_i, 2)
    chip = tp_i // 2
    other = 1 - core
    partner = {"tp": chip * 2 + other}

    def peer(dy):
        return lax.rem(chip + dy, chips)

    def peer_id(dy):
        return {"tp": peer(dy) * 2 + core}

    def share(slot):
        return pl.ds(pl.multiple_of(slot * chan, 16), chan)

    names = ["taps", "wkt", "wup", "wdn", "q", "wko"]
    sources = [
        (taps_hbm, tapst),
        (wkt_hbm, wkt),
        (wup_hbm, wup),
        (wdn_hbm, wdn),
        (q_hbm, qbuf),
        (wko_hbm, wko),
    ]
    loads = {
        name: pltpu.make_async_copy(src, dst, w_sem.at[i])
        for i, (name, (src, dst)) in enumerate(zip(names, sources))
    }
    own_x = [
        pltpu.make_async_copy(x_hbm.at[order[pos]], xg.at[pos, share(tp_i)], w_sem.at[6 + pos])
        for pos in range(places)
    ]
    for c in own_x:
        c.start()
    for name in names:
        loads[name].start()

    barrier = pltpu.get_barrier_semaphore()
    pl.semaphore_signal(barrier, inc=1, device_id=partner, device_id_type=MESH)
    for dy in range(1, chips):
        pl.semaphore_signal(barrier, inc=1, device_id=peer_id(dy), device_id_type=MESH)

    @pl.when(grp_i > 0)
    def _():
        pl.semaphore_signal(barrier, inc=1, device_id={"grp": grp_i - 1}, device_id_type=MESH)

    @pl.when(grp_i < grp_n - 1)
    def _():
        pl.semaphore_signal(barrier, inc=1, device_id={"grp": grp_i + 1}, device_id_type=MESH)

    neighbours = jnp.where(grp_i > 0, 1, 0) + jnp.where(grp_i < grp_n - 1, 1, 0)
    pl.semaphore_wait(barrier, chips + neighbours)

    def rows(ch):
        return pl.ds(ch * rc, rc)

    def x_copy(pos, dy):
        return pltpu.make_async_remote_copy(
            src_ref=x_hbm.at[order[pos]],
            dst_ref=xg.at[pos, share(tp_i)],
            send_sem=x_ssem.at[pos, dy],
            recv_sem=x_rsem.at[pos, dy],
            device_id=peer_id(dy) if dy else partner,
            device_id_type=MESH,
        )

    def x_pass(pos, dy):
        slot = lax.rem(chip - dy + chips, chips) * 2 + core
        return pltpu.make_async_remote_copy(
            src_ref=xg.at[pos, share(slot)],
            dst_ref=xg.at[pos, share(slot)],
            send_sem=xp_ssem.at[pos, dy],
            recv_sem=xp_rsem.at[pos, dy],
            device_id=partner,
            device_id_type=MESH,
        )

    def x_forward(pos):
        for dy in range(1, chips):
            x_copy(pos, dy).wait_recv()
            x_pass(pos, dy).start()

    for pos in range(places):
        for dy in list(range(1, chips)) + [0]:
            x_copy(pos, dy).start()

    kv_cols = kvt.shape[1]
    step = 2 * HD

    def tap_rows(pos):
        taps[pos * tile : (pos + 1) * tile, :] = tapst[order[pos]].T

    tap_blocks = kv_cols // step

    def tap_product(low, high):
        def body(at, carry):
            block = lax.rem(at * kv_heads, tap_blocks) + at * kv_heads // tap_blocks
            cols = pl.ds(pl.multiple_of(block * step, step), step)
            kvt[:, cols] = jnp.dot(taps[...], wkt[:, cols], preferred_element_type=F32)
            return carry

        lax.fori_loop(low, high, body, 0)

    units = hidden.shape[1]

    def layer_norm(pos):
        own_x[pos].wait()
        x_copy(pos, 0).wait_recv()
        for dy in range(1, chips):
            x_pass(pos, dy).wait_recv()
        blocks = [slice(b * HD, (b + 1) * HD) for b in range(depth // HD)]
        total = jnp.zeros((8, tile), F32)
        for b in blocks:
            values = xg[pos, b, :].astype(F32)
            total = total + jnp.sum(values.reshape(HD // 8, 8, tile), axis=0)
        average = jnp.sum(total, axis=0, keepdims=True) / depth
        square = jnp.zeros((8, tile), F32)
        for b in blocks:
            centered = xg[pos, b, :].astype(F32) - average
            square = square + jnp.sum((centered * centered).reshape(HD // 8, 8, tile), axis=0)
        factor = lax.rsqrt(jnp.sum(square, axis=0, keepdims=True) / depth + epsilon)
        for b in blocks:
            scaled = ((xg[pos, b, :].astype(F32) - average) * factor).T
            normed[:, b] = (scaled * gain_ref[b].reshape(1, HD) + bias_ref[b].reshape(1, HD)).astype(
                BF16
            )

    def up(pos):
        if pos == 0:
            loads["wup"].wait()
        for j in range(0, units, 256):
            cols = slice(j, min(j + 256, units))
            pre = jnp.dot(normed[...], wup[:, cols], preferred_element_type=F32)
            pre = pre + bup_ref[cols].reshape(1, -1)
            hidden[:, cols] = (0.5 * pre * (1.0 + lax.erf(pre * (0.5**0.5)))).astype(BF16)

    def down(pos):
        if pos == 0:
            loads["wdn"].wait()
        terms = jnp.dot(hidden[...], wdn[...], preferred_element_type=F32).astype(BF16).T
        for t in range(tp_n):
            m_send[pos, t % 2, t // 2] = terms[t * chan : (t + 1) * chan, :]
        start_l1((0, pos))

    def buffers(stage):
        which, at = stage
        if which == 0:
            return (b.at[at] for b in (m_send, m_r1, m_s2, m_r2))
        return (b.at[at] for b in (k_send, k_r1, k_s2, k_r2))

    def number(stage):
        which, at = stage
        return at if which == 0 else places + at

    def l1(stage, dy):
        send, r1, _, _ = buffers(stage)
        y = peer(dy)
        return pltpu.make_async_remote_copy(
            src_ref=send.at[other, y],
            dst_ref=r1.at[y],
            send_sem=l1_ssem.at[number(stage), dy],
            recv_sem=l1_rsem.at[number(stage), dy],
            device_id=partner,
            device_id_type=MESH,
        )

    def start_l1(stage):
        for dy in list(range(1, chips)) + [0]:
            l1(stage, dy).start()

    def l2(stage, dy):
        _, _, s2, r2 = buffers(stage)
        return pltpu.make_async_remote_copy(
            src_ref=s2.at[dy - 1],
            dst_ref=r2.at[dy - 1],
            send_sem=l2_ssem.at[number(stage), dy - 1],
            recv_sem=l2_rsem.at[number(stage), dy - 1],
            device_id=peer_id(dy),
            device_id_type=MESH,
        )

    def level2(stage):
        send, r1, s2, _ = buffers(stage)
        for dy in range(1, chips):
            y = peer(dy)
            l1(stage, dy).wait_recv()
            s2[dy - 1] = (send[core, y].astype(F32) + r1[y].astype(F32)).astype(BF16)
            l2(stage, dy).start()

    def summed(stage):
        send, r1, _, r2 = buffers(stage)
        l1(stage, 0).wait_recv()
        total = send[core, chip].astype(F32) + r1[chip].astype(F32)
        for dy in range(1, chips):
            l2(stage, dy).wait_recv()
            total = total + r2[dy - 1].astype(F32)
        return total

    def encode(pos):
        here = summed((0, pos)) + xg[pos, share(tp_i), :].astype(F32)
        encoded[pos * tile : (pos + 1) * tile, :] = (
            here.T + bdn_ref[...].reshape(1, chan)
        ).astype(BF16)

    def project(h, ch):
        if h == 0 and ch == 0:
            loads["wko"].wait()
        at = h * nch + ch
        for dy in list(range(1, chips)) + [0]:
            y = peer(dy)
            for side in (other, core):
                start = (lax.div((y * 2 + side) * KVH, tp_n) + h) * step
                cols = pl.ds(pl.multiple_of(start, step), step)
                k_send[at, side, y] = (
                    jnp.dot(encoded[rows(ch), :], wko[:, cols], preferred_element_type=F32)
                    + kvt[rows(ch), cols]
                ).astype(BF16)
                if side is other:
                    l1((1, at), dy).start()

    def finish(h, ch):
        total = summed((1, h * nch + ch))
        key = total[:, :HD]
        square = jnp.mean(key * key, axis=-1, keepdims=True)
        key = (key * lax.rsqrt(square + epsilon) * kgain_ref[...].reshape(1, HD)).astype(BF16)
        value = total[:, HD:].astype(BF16)
        for p in range(per):
            pos = ch * per + p
            at = order[pos] * grp_n + grp_i
            kvs[h][at, :, :HD] = key[p * tile : (p + 1) * tile]
            kvs[h][at, :, HD:] = value[p * tile : (p + 1) * tile]
            z_start(h, pos, 0)

    def reaches_up(index, q):
        return (index >= REQ_G * q) & (index >= total_tiles - CAP * (grp_n - q))

    def reaches_down(index, q):
        return (index < total_tiles - REQ_G * (grp_n - 1 - q)) & (index < CAP * (q + 1))

    def z_copy(h, pos, way, k):
        block = jnp.clip(grp_i - k if way == 0 else grp_i + k, 0, grp_n - 1)
        at = order[pos] * grp_n + block
        return pltpu.make_async_remote_copy(
            src_ref=kvs[h].at[at],
            dst_ref=kvs[h].at[at],
            send_sem=z_ssem.at[h, way, pos, k],
            recv_sem=z_rsem.at[h, way, pos, k],
            device_id={"grp": grp_i + 1 if way == 0 else grp_i - 1},
            device_id_type=MESH,
        )

    def z_sends(pos, way, k):
        base = order[pos] * grp_n
        if way == 0:
            return (grp_i - k >= 0) & (grp_i < grp_n - 1) & reaches_up(base + grp_i - k, grp_i + 1)
        return (grp_i + k <= grp_n - 1) & (grp_i > 0) & reaches_down(base + grp_i + k, grp_i - 1)

    def z_gets(pos, way, k):
        base = order[pos] * grp_n
        if way == 0:
            return (grp_i - k - 1 >= 0) & reaches_up(base + grp_i - k - 1, grp_i)
        return (grp_i + k + 1 <= grp_n - 1) & reaches_down(base + grp_i + k + 1, grp_i)

    def z_start(h, pos, k):
        for way in range(2):

            @pl.when(z_sends(pos, way, k))
            def _(way=way):
                z_copy(h, pos, way, k).start()

    def z_hop(h, pos, k):
        for way in range(2):

            @pl.when(z_gets(pos, way, k))
            def _(way=way):
                z_copy(h, pos, way, k).wait_recv()

        if k + 1 < grp_n - 1:
            z_start(h, pos, k + 1)

    text_rows = qbuf.shape[0]
    q_heads = qbuf.shape[1] // HD
    per_kv = q_heads // kv_heads
    half = text_rows // REQ_G
    window = min(MAXT, total_tiles)

    offset = jnp.int32(0)
    tiles = [jnp.int32(0), jnp.int32(0)]
    texts = [jnp.int32(0), jnp.int32(0)]
    seen = jnp.int32(0)
    for r in range(owner_ref.shape[0]):
        own = owner_ref[r] == grp_i
        offset = offset + jnp.where(owner_ref[r] < grp_i, tiles_ref[r], 0)
        for i in range(REQ_G):
            here = own & (seen == i)
            tiles[i] = jnp.where(here, tiles_ref[r], tiles[i])
            texts[i] = jnp.where(here, text_ref[r], texts[i])
        seen = seen + own.astype(jnp.int32)

    def head_cols(qh):
        return pl.ds(pl.multiple_of(qh * HD, HD), HD)

    def norm_queries(low, high):
        def body(qh, carry):
            query = qbuf[:, head_cols(qh)].astype(F32)
            square = jnp.mean(query * query, axis=-1, keepdims=True)
            gain = qgain_ref[...].reshape(1, HD) * (LOG2E / float(HD) ** 0.5)
            query = query * lax.rsqrt(square + epsilon) * gain
            qrows[...] = query
            qnorm[0, :, head_cols(qh)] = query[:half].astype(BF16)
            qnorm[1, :, head_cols(qh)] = qrows[pl.ds(texts[0], half), :].astype(BF16)
            return carry

        lax.fori_loop(low, high, body, 0)

    def windows(h):
        for i in range(REQ_G):
            low = offset if i == 0 else offset + tiles[0]
            start = jnp.minimum(low, total_tiles - window)
            here = kvs[h][pl.ds(start, window)].reshape(window * tile, 2 * HD)
            row = lax.broadcasted_iota(jnp.int32, (window * tile, HD), 0) + start * tile
            valid = (row >= low * tile) & (row < (low + tiles[i]) * tile)
            kwin[i] = jnp.where(valid, here[:, :HD].astype(F32), 0.0).astype(BF16)
            vwin[i, :, :HD] = jnp.where(valid, here[:, HD:].astype(F32) * V_SCALE, 0.0).astype(BF16)
            vwin[i, :, HD:] = jnp.where(valid, V_SCALE, 0.0).astype(BF16)

    def out_copy(pair):
        cols = pl.ds(pl.multiple_of(pair * 2 * HD, HD), 2 * HD)
        return pltpu.make_async_copy(obuf.at[pair], out_ref.at[:, cols], o_sem.at[pair])

    def attend(low, high):
        row = lax.broadcasted_iota(jnp.int32, (half, 1), 0)
        both = texts[0] + texts[1]
        first = row < texts[0]
        top, bottom = row < both, row + half < both

        def request(qh, i):
            scores = lax.dot_general(
                qnorm[i, :, head_cols(qh)],
                kwin[i],
                (((1,), (1,)), ((), ())),
                preferred_element_type=F32,
            )
            weights = jnp.exp2(scores).astype(BF16)
            result = jnp.dot(weights, vwin[i], preferred_element_type=F32)
            return result[:, :HD] / result[:, HD:]

        def body(pair, carry):
            for slot in range(2):
                qh = pair * 2 + slot
                orows[slot, half : 2 * half] = request(qh, 1)
                moved = orows[slot, pl.ds(half - texts[0], text_rows)]
                mine = request(qh, 0)
                inside = slice(slot * HD, (slot + 1) * HD)
                obuf[pair, :half, inside] = jnp.where(
                    first, mine, jnp.where(top, moved[:half], 0.0)
                ).astype(BF16)
                obuf[pair, half:, inside] = jnp.where(bottom, moved[half:], 0.0).astype(BF16)
            out_copy(pair).start()
            return carry

        lax.fori_loop(low, high, body, 0)

    loads["taps"].wait()
    for pos in range(places):
        tap_rows(pos)
    loads["wkt"].wait()

    ready = tap_blocks // kv_heads
    tap_product(0, tap_blocks // 2)
    x_forward(0)
    for pos in range(places):
        layer_norm(pos)
        up(pos)
        if pos > 0:
            level2((0, pos - 1))
        if pos + 1 < places:
            x_forward(pos + 1)
        down(pos)
    tapped = tap_blocks // 2 + 1
    tap_product(tap_blocks // 2, tapped)
    level2((0, places - 1))
    if tapped < ready:
        tap_product(tapped, ready)
        tapped = ready

    stages = [(h, ch) for h in range(kv_heads) for ch in range(nch)]
    sent = 0
    for ch in range(nch):
        for pos in range(ch * per, (ch + 1) * per):
            encode(pos)
        project(0, ch)
        if ch < nch - 1:
            level2((1, ch))
            sent += 1
        if ch == 0 and tapped < tap_blocks:
            tap_product(tapped, tap_blocks)
        if ch == nch - 1:
            for h in range(1, kv_heads):
                project(h, 0)
                level2((1, sent))
                sent += 1
                for later in range(1, nch):
                    project(h, later)
    for j in range(sent, len(stages)):
        level2((1, j))
    loads["q"].wait()
    norm_queries(0, per_kv)

    last = grp_n - 2

    def chunk(ch):
        return range(ch * per, (ch + 1) * per)

    for h in range(kv_heads):
        if h == 0:
            for ch in range(nch):
                finish(0, ch)
                if ch == 0:
                    norm_queries(per_kv, q_heads)
            for k in range(last):
                for pos in range(places):
                    z_hop(0, pos, k)
                for ch in range(nch):
                    if kv_heads > 1 and k == ch:
                        finish(1, ch)
        if h == 0 and kv_heads > 1:
            for ch in range(last, nch):
                finish(1, ch)
        for pos in range(places):
            z_hop(h, pos, last)
        windows(h)
        base = h * per_kv
        if h + 1 < kv_heads:
            parts = last + 1
            edges = [(base + per_kv * p // parts) // 2 for p in range(parts + 1)]
            for k in range(parts):
                attend(edges[k], edges[k + 1])
                if k < last:
                    for pos in range(places):
                        z_hop(h + 1, pos, k)
        else:
            attend(base // 2, (base + per_kv) // 2)

    for pos in range(places):
        for dy in range(chips):
            x_copy(pos, dy).wait_send()
        for dy in range(1, chips):
            x_pass(pos, dy).wait_send()
    for stage in [(0, pos) for pos in range(places)] + [(1, j) for j in range(len(stages))]:
        for dy in range(chips):
            l1(stage, dy).wait_send()
        for dy in range(1, chips):
            l2(stage, dy).wait_send()
    for h in range(kv_heads):
        for pos in range(places):
            for k in range(grp_n - 1):
                for way in range(2):

                    @pl.when(z_sends(pos, way, k))
                    def _(h=h, pos=pos, way=way, k=k):
                        z_copy(h, pos, way, k).wait_send()
    for pair in range(q_heads // 2):
        out_copy(pair).wait()


def local(
    x_in,
    taps,
    ln_gain,
    ln_bias,
    w_up,
    b_up,
    w_down,
    b_down,
    kv_w_out,
    kv_w_taps,
    k_gain,
    q_gain,
    queries,
    tiles_per_request,
    owner,
    text_per_request,
):
    grp_n = lax.axis_size("grp")
    tp_n = lax.axis_size("tp")
    chips = tp_n // 2
    places, _, tile, chan = x_in.shape
    n = places * tile
    nch = 2 if places % 2 == 0 else 1
    rc = n // nch
    depth, units = w_up.shape
    tap_share, kv_cols = kv_w_taps.shape
    kv_heads = max(1, KVH // tp_n)
    width = 2 * HD
    stages = kv_heads * nch
    text_rows, query_width = queries.shape
    half = text_rows // REQ_G
    window = min(MAXT, places * grp_n) * tile
    any_spec = pl.BlockSpec(memory_space=pl.ANY)
    vmem_spec = pl.BlockSpec(memory_space=pltpu.VMEM)
    smem_spec = pl.BlockSpec(memory_space=pltpu.SMEM)
    dma = pltpu.SemaphoreType.DMA
    return pl.pallas_call(
        functools.partial(fused_kernel, (tp_n, grp_n, nch, chan, kv_heads)),
        name="fused",
        out_shape=pltpu.VMEM(queries.shape, BF16),
        in_specs=[
            any_spec,
            any_spec,
            vmem_spec,
            vmem_spec,
            any_spec,
            vmem_spec,
            any_spec,
            vmem_spec,
            any_spec,
            any_spec,
            vmem_spec,
            vmem_spec,
            any_spec,
            smem_spec,
            smem_spec,
            smem_spec,
        ],
        out_specs=any_spec,
        scratch_shapes=[
            pltpu.VMEM((places, depth, tile), BF16),
            pltpu.VMEM((tile, depth), BF16),
            pltpu.VMEM((tile, units), BF16),
            pltpu.VMEM((places, tap_share, tile), BF16),
            pltpu.VMEM((n, tap_share), BF16),
            pltpu.VMEM(w_up.shape, BF16),
            pltpu.VMEM(w_down.shape, BF16),
            pltpu.VMEM(kv_w_out.shape, BF16),
            pltpu.VMEM(kv_w_taps.shape, BF16),
            pltpu.VMEM((n, kv_cols), F32),
            pltpu.VMEM((n, chan), BF16),
            pltpu.VMEM((places, 2, chips, chan, tile), BF16),
            pltpu.VMEM((places, chips, chan, tile), BF16),
            pltpu.VMEM((places, chips - 1, chan, tile), BF16),
            pltpu.VMEM((places, chips - 1, chan, tile), BF16),
            pltpu.VMEM((stages, 2, chips, rc, width), BF16),
            pltpu.VMEM((stages, chips, rc, width), BF16),
            pltpu.VMEM((stages, chips - 1, rc, width), BF16),
            pltpu.VMEM((stages, chips - 1, rc, width), BF16),
            pltpu.VMEM((REQ_G, window, HD), BF16),
            pltpu.VMEM((REQ_G, window, 2 * HD), BF16),
            pltpu.VMEM((text_rows, query_width), BF16),
            pltpu.VMEM((REQ_G, half, query_width), BF16),
            pltpu.VMEM((text_rows, HD), F32),
            pltpu.VMEM((2, half + text_rows, HD), F32),
            pltpu.VMEM((query_width // (2 * HD), text_rows, 2 * HD), BF16),
        ]
        + [pltpu.VMEM((places * grp_n, tile, width), BF16) for _ in range(kv_heads)]
        + [
            dma((6 + places,)),
            dma((places, chips)),
            dma((places, chips)),
            dma((places, chips)),
            dma((places, chips)),
            dma((places + stages, chips)),
            dma((places + stages, chips)),
            dma((places + stages, chips - 1)),
            dma((places + stages, chips - 1)),
            dma((kv_heads, 2, places, grp_n - 1)),
            dma((kv_heads, 2, places, grp_n - 1)),
            dma((query_width // (2 * HD),)),
        ],
        compiler_params=pltpu.CompilerParams(
            collective_id=0, has_side_effects=True, vmem_limit_bytes=VMEM_BYTES
        ),
    )(
        jnp.transpose(x_in, (0, 1, 3, 2)).reshape(places, chan, tile),
        jnp.transpose(taps, (0, 1, 3, 2)).reshape(places, tap_share, tile),
        ln_gain,
        ln_bias,
        w_up,
        b_up,
        w_down,
        b_down,
        kv_w_out,
        kv_w_taps,
        k_gain,
        q_gain,
        queries,
        tiles_per_request,
        owner,
        text_per_request,
    )


def solution(mesh):
    in_specs = (
        P(None, ("rep", "grp"), None, "tp"),
        P(None, ("rep", "grp"), None, "tp"),
        P(),
        P(),
        P(None, "tp"),
        P("tp"),
        P("tp", None),
        P("tp"),
        P("tp", None),
        P("tp", None),
        P(),
        P(),
        P(("rep", "grp"), "tp"),
        P("rep"),
        P("rep"),
        P("rep"),
    )
    out_specs = P(("rep", "grp"), "tp")
    return jax.shard_map(local, mesh=mesh, in_specs=in_specs, out_specs=out_specs, check_vma=False)
```

```python
import functools

import jax
import jax.numpy as jnp
from jax import lax
from jax.experimental import pallas as pl
from jax.experimental.pallas import tpu as pltpu
from jax.sharding import PartitionSpec as P

KVH = 8
HD = 128
MAXT = 4
REQ_G = 2
CAP = REQ_G * MAXT

epsilon = 1e-05
MESH = pl.DeviceIdType.MESH
VMEM_BYTES = 60 * 1024 * 1024
LOG2E = 1.4426950408889634
V_SCALE = 2.0**-14
F32 = jnp.float32
BF16 = jnp.bfloat16


def fused_kernel(
    sizes,
    x_hbm,
    taps_hbm,
    gain_hbm,
    bias_hbm,
    wup_hbm,
    bup_hbm,
    wdn_hbm,
    bdn_hbm,
    wko_hbm,
    wkt_hbm,
    kgain_hbm,
    qgain_hbm,
    q_hbm,
    tiles_ref,
    owner_ref,
    text_ref,
    out_ref,
    xg,
    normed,
    hidden,
    tapst,
    taps,
    wup,
    wdn,
    wko,
    wkt,
    kvt,
    encoded,
    m_send,
    m_r1,
    m_s2,
    m_r2,
    k_send,
    k_r1,
    k_s2,
    k_r2,
    kwin,
    vwin,
    qbuf,
    qnorm,
    qrows,
    orows,
    obuf,
    gain_ref,
    bias_ref,
    bup_ref,
    bdn_ref,
    kgain_ref,
    qgain_ref,
    *rest,
):
    tp_n, grp_n, nch, chan, kv_heads = sizes
    kvs, sems = rest[:kv_heads], rest[kv_heads:]
    (
        w_sem,
        x_ssem,
        x_rsem,
        xp_ssem,
        xp_rsem,
        l1_ssem,
        l1_rsem,
        l2_ssem,
        l2_rsem,
        z_ssem,
        z_rsem,
        o_sem,
        s_sem,
    ) = sems
    places, depth, tile = xg.shape
    total_tiles = places * grp_n
    per = places // nch
    rc = per * tile
    chips = tp_n // 2
    order = sorted(range(places), key=lambda k: (abs(2 * k - (places - 1)), k))
    tp_i = lax.axis_index("tp")
    grp_i = lax.axis_index("grp")
    core = lax.rem(tp_i, 2)
    chip = tp_i // 2
    other = 1 - core
    partner = {"tp": chip * 2 + other}

    def peer(dy):
        return lax.rem(chip + dy, chips)

    def peer_id(dy):
        return {"tp": peer(dy) * 2 + core}

    def share(slot):
        return pl.ds(pl.multiple_of(slot * chan, 16), chan)

    names = ["taps", "wkt", "wup", "wdn", "q", "wko"]
    sources = [
        (taps_hbm, tapst),
        (wkt_hbm, wkt),
        (wup_hbm, wup),
        (wdn_hbm, wdn),
        (q_hbm, qbuf),
        (wko_hbm, wko),
    ]
    loads = {
        name: pltpu.make_async_copy(src, dst, w_sem.at[i])
        for i, (name, (src, dst)) in enumerate(zip(names, sources))
    }
    own_x = [
        pltpu.make_async_copy(x_hbm.at[order[pos]], xg.at[pos, share(tp_i)], w_sem.at[6 + pos])
        for pos in range(places)
    ]
    small = [
        pltpu.make_async_copy(src, dst, s_sem.at[i])
        for i, (src, dst) in enumerate(
            [
                (gain_hbm, gain_ref),
                (bias_hbm, bias_ref),
                (bup_hbm, bup_ref),
                (bdn_hbm, bdn_ref),
                (kgain_hbm, kgain_ref),
                (qgain_hbm, qgain_ref),
            ]
        )
    ]

    barrier = pltpu.get_barrier_semaphore()
    pl.semaphore_signal(barrier, inc=1, device_id=partner, device_id_type=MESH)
    for dy in range(1, chips):
        pl.semaphore_signal(barrier, inc=1, device_id=peer_id(dy), device_id_type=MESH)

    @pl.when(grp_i > 0)
    def _():
        pl.semaphore_signal(barrier, inc=1, device_id={"grp": grp_i - 1}, device_id_type=MESH)

    @pl.when(grp_i < grp_n - 1)
    def _():
        pl.semaphore_signal(barrier, inc=1, device_id={"grp": grp_i + 1}, device_id_type=MESH)

    for c in own_x + small:
        c.start()
    for name in names:
        loads[name].start()
    neighbours = jnp.where(grp_i > 0, 1, 0) + jnp.where(grp_i < grp_n - 1, 1, 0)
    pl.semaphore_wait(barrier, chips + neighbours)

    def rows(ch):
        return pl.ds(ch * rc, rc)

    def x_copy(pos, dy):
        return pltpu.make_async_remote_copy(
            src_ref=x_hbm.at[order[pos]],
            dst_ref=xg.at[pos, share(tp_i)],
            send_sem=x_ssem.at[pos, dy],
            recv_sem=x_rsem.at[pos, dy],
            device_id=peer_id(dy) if dy else partner,
            device_id_type=MESH,
        )

    def x_pass(pos, dy):
        slot = lax.rem(chip - dy + chips, chips) * 2 + core
        return pltpu.make_async_remote_copy(
            src_ref=xg.at[pos, share(slot)],
            dst_ref=xg.at[pos, share(slot)],
            send_sem=xp_ssem.at[pos, dy],
            recv_sem=xp_rsem.at[pos, dy],
            device_id=partner,
            device_id_type=MESH,
        )

    def x_forward(pos):
        for dy in range(1, chips):
            x_copy(pos, dy).wait_recv()
            x_pass(pos, dy).start()

    for pos in range(places):
        for dy in list(range(1, chips)) + [0]:
            x_copy(pos, dy).start()

    kv_cols = kvt.shape[1]
    step = 2 * HD

    def tap_rows(pos):
        taps[pos * tile : (pos + 1) * tile, :] = tapst[order[pos]].T

    tap_blocks = kv_cols // step

    def tap_product(low, high):
        def body(at, carry):
            block = lax.rem(at * kv_heads, tap_blocks) + at * kv_heads // tap_blocks
            cols = pl.ds(pl.multiple_of(block * step, step), step)
            kvt[:, cols] = jnp.dot(taps[...], wkt[:, cols], preferred_element_type=F32)
            return carry

        lax.fori_loop(low, high, body, 0)

    units = hidden.shape[1]

    def layer_norm(pos):
        own_x[pos].wait()
        x_copy(pos, 0).wait_recv()
        for dy in range(1, chips):
            x_pass(pos, dy).wait_recv()
        blocks = [slice(b * HD, (b + 1) * HD) for b in range(depth // HD)]
        total = jnp.zeros((8, tile), F32)
        for b in blocks:
            values = xg[pos, b, :].astype(F32)
            total = total + jnp.sum(values.reshape(HD // 8, 8, tile), axis=0)
        average = jnp.sum(total, axis=0, keepdims=True) / depth
        square = jnp.zeros((8, tile), F32)
        for b in blocks:
            centered = xg[pos, b, :].astype(F32) - average
            square = square + jnp.sum((centered * centered).reshape(HD // 8, 8, tile), axis=0)
        factor = lax.rsqrt(jnp.sum(square, axis=0, keepdims=True) / depth + epsilon)
        for b in blocks:
            scaled = ((xg[pos, b, :].astype(F32) - average) * factor).T
            normed[:, b] = (scaled * gain_ref[b].reshape(1, HD) + bias_ref[b].reshape(1, HD)).astype(
                BF16
            )

    def up(pos):
        if pos == 0:
            loads["wup"].wait()
        for j in range(0, units, 256):
            cols = slice(j, min(j + 256, units))
            pre = jnp.dot(normed[...], wup[:, cols], preferred_element_type=F32)
            pre = pre + bup_ref[cols].reshape(1, -1)
            hidden[:, cols] = (0.5 * pre * (1.0 + lax.erf(pre * (0.5**0.5)))).astype(BF16)

    def down(pos):
        if pos == 0:
            loads["wdn"].wait()
        terms = jnp.dot(hidden[...], wdn[...], preferred_element_type=F32).astype(BF16).T
        for t in range(tp_n):
            m_send[pos, t % 2, t // 2] = terms[t * chan : (t + 1) * chan, :]
        start_l1((0, pos))

    def buffers(stage):
        which, at = stage
        if which == 0:
            return (b.at[at] for b in (m_send, m_r1, m_s2, m_r2))
        return (b.at[at] for b in (k_send, k_r1, k_s2, k_r2))

    def number(stage):
        which, at = stage
        return at if which == 0 else places + at

    def l1(stage, dy):
        send, r1, _, _ = buffers(stage)
        y = peer(dy)
        return pltpu.make_async_remote_copy(
            src_ref=send.at[other, y],
            dst_ref=r1.at[y],
            send_sem=l1_ssem.at[number(stage), dy],
            recv_sem=l1_rsem.at[number(stage), dy],
            device_id=partner,
            device_id_type=MESH,
        )

    def start_l1(stage):
        for dy in list(range(1, chips)) + [0]:
            l1(stage, dy).start()

    def l2(stage, dy):
        _, _, s2, r2 = buffers(stage)
        return pltpu.make_async_remote_copy(
            src_ref=s2.at[dy - 1],
            dst_ref=r2.at[dy - 1],
            send_sem=l2_ssem.at[number(stage), dy - 1],
            recv_sem=l2_rsem.at[number(stage), dy - 1],
            device_id=peer_id(dy),
            device_id_type=MESH,
        )

    def level2(stage):
        send, r1, s2, _ = buffers(stage)
        for dy in range(1, chips):
            y = peer(dy)
            l1(stage, dy).wait_recv()
            s2[dy - 1] = (send[core, y].astype(F32) + r1[y].astype(F32)).astype(BF16)
            l2(stage, dy).start()

    def summed(stage):
        send, r1, _, r2 = buffers(stage)
        l1(stage, 0).wait_recv()
        total = send[core, chip].astype(F32) + r1[chip].astype(F32)
        for dy in range(1, chips):
            l2(stage, dy).wait_recv()
            total = total + r2[dy - 1].astype(F32)
        return total

    def encode(pos):
        here = summed((0, pos)) + xg[pos, share(tp_i), :].astype(F32)
        encoded[pos * tile : (pos + 1) * tile, :] = (
            here.T + bdn_ref[...].reshape(1, chan)
        ).astype(BF16)

    def project(h, ch):
        if h == 0 and ch == 0:
            loads["wko"].wait()
        at = h * nch + ch
        for dy in list(range(1, chips)) + [0]:
            y = peer(dy)
            for side in (other, core):
                start = (lax.div((y * 2 + side) * KVH, tp_n) + h) * step
                cols = pl.ds(pl.multiple_of(start, step), step)
                k_send[at, side, y] = (
                    jnp.dot(encoded[rows(ch), :], wko[:, cols], preferred_element_type=F32)
                    + kvt[rows(ch), cols]
                ).astype(BF16)
                if side is other:
                    l1((1, at), dy).start()

    def finish(h, ch):
        total = summed((1, h * nch + ch))
        key = total[:, :HD]
        square = jnp.mean(key * key, axis=-1, keepdims=True)
        key = (key * lax.rsqrt(square + epsilon) * kgain_ref[...].reshape(1, HD)).astype(BF16)
        value = total[:, HD:].astype(BF16)
        for p in range(per):
            pos = ch * per + p
            at = order[pos] * grp_n + grp_i
            kvs[h][at, :, :HD] = key[p * tile : (p + 1) * tile]
            kvs[h][at, :, HD:] = value[p * tile : (p + 1) * tile]
        for pos, way in travels(h):
            if pos // per == ch:
                z_start(h, pos, way, 0)

    def reaches_up(index, q):
        return (index >= REQ_G * q) & (index >= total_tiles - CAP * (grp_n - q))

    def reaches_down(index, q):
        return (index < total_tiles - REQ_G * (grp_n - 1 - q)) & (index < CAP * (q + 1))

    def z_copy(h, pos, way, k):
        block = jnp.clip(grp_i - k if way == 0 else grp_i + k, 0, grp_n - 1)
        at = order[pos] * grp_n + block
        return pltpu.make_async_remote_copy(
            src_ref=kvs[h].at[at],
            dst_ref=kvs[h].at[at],
            send_sem=z_ssem.at[h, way, pos, k],
            recv_sem=z_rsem.at[h, way, pos, k],
            device_id={"grp": grp_i + 1 if way == 0 else grp_i - 1},
            device_id_type=MESH,
        )

    def z_sends(pos, way, k):
        base = order[pos] * grp_n
        if way == 0:
            return (grp_i - k >= 0) & (grp_i < grp_n - 1) & reaches_up(base + grp_i - k, grp_i + 1)
        return (grp_i + k <= grp_n - 1) & (grp_i > 0) & reaches_down(base + grp_i + k, grp_i - 1)

    def z_gets(pos, way, k):
        base = order[pos] * grp_n
        if way == 0:
            return (grp_i - k - 1 >= 0) & reaches_up(base + grp_i - k - 1, grp_i)
        return (grp_i + k + 1 <= grp_n - 1) & reaches_down(base + grp_i + k + 1, grp_i)

    def z_start(h, pos, way, k):
        @pl.when(z_sends(pos, way, k))
        def _():
            z_copy(h, pos, way, k).start()

    def chunks(h):
        return range(nch) if h == 0 else range(nch - 1, -1, -1)

    def travels(h):
        found = []
        for ch in chunks(h):
            here = list(range(ch * per, (ch + 1) * per))
            up_way = sorted(here, key=lambda pos: -order[pos])
            down_way = sorted(here, key=lambda pos: order[pos])
            for p in range(per):
                found += [(up_way[p], 0), (down_way[p], 1)]
        return found

    def z_hop(h, k):
        for pos, way in travels(h):

            @pl.when(z_gets(pos, way, k))
            def _(pos=pos, way=way):
                z_copy(h, pos, way, k).wait_recv()

            if k + 1 < grp_n - 1:
                z_start(h, pos, way, k + 1)

    text_rows = qbuf.shape[0]
    q_heads = qbuf.shape[1] // HD
    per_kv = q_heads // kv_heads
    half = text_rows // REQ_G
    window = min(MAXT, total_tiles)

    offset = jnp.int32(0)
    tiles = [jnp.int32(0), jnp.int32(0)]
    texts = [jnp.int32(0), jnp.int32(0)]
    seen = jnp.int32(0)
    for r in range(owner_ref.shape[0]):
        own = owner_ref[r] == grp_i
        offset = offset + jnp.where(owner_ref[r] < grp_i, tiles_ref[r], 0)
        for i in range(REQ_G):
            here = own & (seen == i)
            tiles[i] = jnp.where(here, tiles_ref[r], tiles[i])
            texts[i] = jnp.where(here, text_ref[r], texts[i])
        seen = seen + own.astype(jnp.int32)

    def head_cols(qh):
        return pl.ds(pl.multiple_of(qh * HD, HD), HD)

    def norm_queries(low, high):
        def body(qh, carry):
            query = qbuf[:, head_cols(qh)].astype(F32)
            square = jnp.mean(query * query, axis=-1, keepdims=True)
            gain = qgain_ref[...].reshape(1, HD) * (LOG2E / float(HD) ** 0.5)
            query = query * lax.rsqrt(square + epsilon) * gain
            qrows[...] = query
            qnorm[0, :, head_cols(qh)] = query[:half].astype(BF16)
            qnorm[1, :, head_cols(qh)] = qrows[pl.ds(texts[0], half), :].astype(BF16)
            return carry

        lax.fori_loop(low, high, body, 0)

    def windows(h):
        for i in range(REQ_G):
            low = offset if i == 0 else offset + tiles[0]
            start = jnp.minimum(low, total_tiles - window)
            here = kvs[h][pl.ds(start, window)].reshape(window * tile, 2 * HD)
            row = lax.broadcasted_iota(jnp.int32, (window * tile, HD), 0) + start * tile
            valid = (row >= low * tile) & (row < (low + tiles[i]) * tile)
            kwin[i] = jnp.where(valid, here[:, :HD].astype(F32), 0.0).astype(BF16)
            vwin[i, :, :HD] = jnp.where(valid, here[:, HD:].astype(F32) * V_SCALE, 0.0).astype(BF16)
            vwin[i, :, HD:] = jnp.where(valid, V_SCALE, 0.0).astype(BF16)

    def out_copy(pair):
        cols = pl.ds(pl.multiple_of(pair * 2 * HD, HD), 2 * HD)
        return pltpu.make_async_copy(obuf.at[pair], out_ref.at[:, cols], o_sem.at[pair])

    def attend(low, high):
        row = lax.broadcasted_iota(jnp.int32, (half, 1), 0)
        both = texts[0] + texts[1]
        first = row < texts[0]
        top, bottom = row < both, row + half < both

        def request(qh, i):
            scores = lax.dot_general(
                qnorm[i, :, head_cols(qh)],
                kwin[i],
                (((1,), (1,)), ((), ())),
                preferred_element_type=F32,
            )
            weights = jnp.exp2(scores).astype(BF16)
            result = jnp.dot(weights, vwin[i], preferred_element_type=F32)
            return result[:, :HD] / result[:, HD:]

        def body(pair, carry):
            for slot in range(2):
                qh = pair * 2 + slot
                orows[slot, half : 2 * half] = request(qh, 1)
                moved = orows[slot, pl.ds(half - texts[0], text_rows)]
                mine = request(qh, 0)
                inside = slice(slot * HD, (slot + 1) * HD)
                obuf[pair, :half, inside] = jnp.where(
                    first, mine, jnp.where(top, moved[:half], 0.0)
                ).astype(BF16)
                obuf[pair, half:, inside] = jnp.where(bottom, moved[half:], 0.0).astype(BF16)
            out_copy(pair).start()
            return carry

        lax.fori_loop(low, high, body, 0)

    for c in small:
        c.wait()
    loads["taps"].wait()
    for pos in range(places):
        tap_rows(pos)
    loads["wkt"].wait()

    ready = tap_blocks // kv_heads
    tap_product(0, tap_blocks // 2)
    x_forward(0)
    for pos in range(places):
        layer_norm(pos)
        up(pos)
        if pos > 0:
            level2((0, pos - 1))
        if pos + 1 < places:
            x_forward(pos + 1)
        down(pos)
    tapped = tap_blocks // 2 + 1
    tap_product(tap_blocks // 2, tapped)
    level2((0, places - 1))
    if tapped < ready:
        tap_product(tapped, ready)
        tapped = ready

    def more_taps(count):
        nonlocal tapped
        count = min(count, tap_blocks - tapped)
        if count > 0:
            tap_product(tapped, tapped + count)
            tapped += count

    def encode_chunk(ch):
        for pos in range(ch * per, (ch + 1) * per):
            encode(pos)

    stages = [(h, ch) for h in range(kv_heads) for ch in range(nch)]
    encode_chunk(0)
    project(0, 0)
    more_taps(1)
    level2((1, 0))
    for ch in range(1, nch):
        encode_chunk(ch)
        project(0, ch)
        more_taps(1)
        level2((1, ch))
    more_taps(tap_blocks)
    pending = [(h, ch) for h in range(1, kv_heads) for ch in chunks(h)]
    if pending:
        project(*pending[0])
    finish(0, 0)
    for j, (h, ch) in enumerate(pending):
        if j + 1 < len(pending):
            project(*pending[j + 1])
        level2((1, h * nch + ch))
    loads["q"].wait()
    norm_queries(0, per_kv)
    for ch in range(1, nch):
        finish(0, ch)
    last = grp_n - 2
    for h in range(kv_heads):
        if h == 0:
            coming = pending[:nch]
            for k in range(last):
                z_hop(0, k)
                if k == 0:
                    norm_queries(per_kv, q_heads)
                if coming:
                    finish(*coming.pop(0))
            while coming:
                finish(*coming.pop(0))
        z_hop(h, last)
        windows(h)
        base = h * per_kv
        if h + 1 < kv_heads:
            parts = last + 1
            edges = [(base + per_kv * p // parts) // 2 for p in range(parts + 1)]
            for k in range(parts):
                attend(edges[k], edges[k + 1])
                if k < last:
                    z_hop(h + 1, k)
        else:
            attend(base // 2, (base + per_kv) // 2)

    for pos in range(places):
        for dy in range(chips):
            x_copy(pos, dy).wait_send()
        for dy in range(1, chips):
            x_pass(pos, dy).wait_send()
    for stage in [(0, pos) for pos in range(places)] + [(1, j) for j in range(len(stages))]:
        for dy in range(chips):
            l1(stage, dy).wait_send()
        for dy in range(1, chips):
            l2(stage, dy).wait_send()
    for h in range(kv_heads):
        for pos in range(places):
            for k in range(grp_n - 1):
                for way in range(2):

                    @pl.when(z_sends(pos, way, k))
                    def _(h=h, pos=pos, way=way, k=k):
                        z_copy(h, pos, way, k).wait_send()
    for pair in range(q_heads // 2):
        out_copy(pair).wait()


def local(
    x_in,
    taps,
    ln_gain,
    ln_bias,
    w_up,
    b_up,
    w_down,
    b_down,
    kv_w_out,
    kv_w_taps,
    k_gain,
    q_gain,
    queries,
    tiles_per_request,
    owner,
    text_per_request,
):
    grp_n = lax.axis_size("grp")
    tp_n = lax.axis_size("tp")
    chips = tp_n // 2
    places, _, tile, chan = x_in.shape
    n = places * tile
    nch = 2 if places % 2 == 0 else 1
    rc = n // nch
    depth, units = w_up.shape
    tap_share, kv_cols = kv_w_taps.shape
    kv_heads = max(1, KVH // tp_n)
    width = 2 * HD
    stages = kv_heads * nch
    text_rows, query_width = queries.shape
    half = text_rows // REQ_G
    window = min(MAXT, places * grp_n) * tile
    any_spec = pl.BlockSpec(memory_space=pl.ANY)
    smem_spec = pl.BlockSpec(memory_space=pltpu.SMEM)
    dma = pltpu.SemaphoreType.DMA
    return pl.pallas_call(
        functools.partial(fused_kernel, (tp_n, grp_n, nch, chan, kv_heads)),
        name="fused",
        out_shape=pltpu.VMEM(queries.shape, BF16),
        in_specs=[
            *[any_spec] * 13,
            smem_spec,
            smem_spec,
            smem_spec,
        ],
        out_specs=any_spec,
        scratch_shapes=[
            pltpu.VMEM((places, depth, tile), BF16),
            pltpu.VMEM((tile, depth), BF16),
            pltpu.VMEM((tile, units), BF16),
            pltpu.VMEM((places, tap_share, tile), BF16),
            pltpu.VMEM((n, tap_share), BF16),
            pltpu.VMEM(w_up.shape, BF16),
            pltpu.VMEM(w_down.shape, BF16),
            pltpu.VMEM(kv_w_out.shape, BF16),
            pltpu.VMEM(kv_w_taps.shape, BF16),
            pltpu.VMEM((n, kv_cols), F32),
            pltpu.VMEM((n, chan), BF16),
            pltpu.VMEM((places, 2, chips, chan, tile), BF16),
            pltpu.VMEM((places, chips, chan, tile), BF16),
            pltpu.VMEM((places, chips - 1, chan, tile), BF16),
            pltpu.VMEM((places, chips - 1, chan, tile), BF16),
            pltpu.VMEM((stages, 2, chips, rc, width), BF16),
            pltpu.VMEM((stages, chips, rc, width), BF16),
            pltpu.VMEM((stages, chips - 1, rc, width), BF16),
            pltpu.VMEM((stages, chips - 1, rc, width), BF16),
            pltpu.VMEM((REQ_G, window, HD), BF16),
            pltpu.VMEM((REQ_G, window, 2 * HD), BF16),
            pltpu.VMEM((text_rows, query_width), BF16),
            pltpu.VMEM((REQ_G, half, query_width), BF16),
            pltpu.VMEM((text_rows, HD), F32),
            pltpu.VMEM((2, half + text_rows, HD), F32),
            pltpu.VMEM((query_width // (2 * HD), text_rows, 2 * HD), BF16),
        ]
        + [pltpu.VMEM(a.shape, F32) for a in (ln_gain, ln_bias, b_up, b_down, k_gain, q_gain)]
        + [pltpu.VMEM((places * grp_n, tile, width), BF16) for _ in range(kv_heads)]
        + [
            dma((6 + places,)),
            dma((places, chips)),
            dma((places, chips)),
            dma((places, chips)),
            dma((places, chips)),
            dma((places + stages, chips)),
            dma((places + stages, chips)),
            dma((places + stages, chips - 1)),
            dma((places + stages, chips - 1)),
            dma((kv_heads, 2, places, grp_n - 1)),
            dma((kv_heads, 2, places, grp_n - 1)),
            dma((query_width // (2 * HD),)),
            dma((6,)),
        ],
        compiler_params=pltpu.CompilerParams(
            collective_id=0, has_side_effects=True, vmem_limit_bytes=VMEM_BYTES
        ),
    )(
        jnp.transpose(x_in, (0, 1, 3, 2)).reshape(places, chan, tile),
        jnp.transpose(taps, (0, 1, 3, 2)).reshape(places, tap_share, tile),
        ln_gain,
        ln_bias,
        w_up,
        b_up,
        w_down,
        b_down,
        kv_w_out,
        kv_w_taps,
        k_gain,
        q_gain,
        queries,
        tiles_per_request,
        owner,
        text_per_request,
    )


def solution(mesh):
    in_specs = (
        P(None, ("rep", "grp"), None, "tp"),
        P(None, ("rep", "grp"), None, "tp"),
        P(),
        P(),
        P(None, "tp"),
        P("tp"),
        P("tp", None),
        P("tp"),
        P("tp", None),
        P("tp", None),
        P(),
        P(),
        P(("rep", "grp"), "tp"),
        P("rep"),
        P("rep"),
        P("rep"),
    )
    out_specs = P(("rep", "grp"), "tp")
    return jax.shard_map(local, mesh=mesh, in_specs=in_specs, out_specs=out_specs, check_vma=False)
```

```python
import functools

import jax
import jax.numpy as jnp
from jax import lax
from jax.experimental import pallas as pl
from jax.experimental.pallas import tpu as pltpu
from jax.sharding import PartitionSpec as P

KVH = 8
HD = 128
MAXT = 4
REQ_G = 2
CAP = REQ_G * MAXT

epsilon = 1e-05
MESH = pl.DeviceIdType.MESH
VMEM_BYTES = 60 * 1024 * 1024
LOG2E = 1.4426950408889634
V_SCALE = 2.0**-14
F32 = jnp.float32
BF16 = jnp.bfloat16


def fused_kernel(
    sizes,
    x_hbm,
    taps_hbm,
    gain_ref,
    bias_ref,
    wup_hbm,
    bup_ref,
    wdn_hbm,
    bdn_ref,
    wko_hbm,
    wkt_hbm,
    kgain_ref,
    qgain_ref,
    q_hbm,
    tiles_ref,
    owner_ref,
    text_ref,
    out_ref,
    xg,
    normed,
    hidden,
    tapst,
    taps,
    wup,
    wdn,
    wko,
    wkt,
    kvt,
    encoded,
    m_send,
    m_r1,
    m_s2,
    m_r2,
    k_send,
    k_r1,
    k_s2,
    k_r2,
    kwin,
    vwin,
    qbuf,
    qnorm,
    qrows,
    orows,
    obuf,
    *rest,
):
    tp_n, grp_n, nch, chan, kv_heads = sizes
    kvs, sems = rest[:kv_heads], rest[kv_heads:]
    (
        w_sem,
        x_ssem,
        x_rsem,
        xp_ssem,
        xp_rsem,
        l1_ssem,
        l1_rsem,
        l2_ssem,
        l2_rsem,
        z_ssem,
        z_rsem,
        o_sem,
    ) = sems
    places, depth, tile = xg.shape
    total_tiles = places * grp_n
    per = places // nch
    rc = per * tile
    chips = tp_n // 2
    order = sorted(range(places), key=lambda k: (abs(2 * k - (places - 1)), k))
    tp_i = lax.axis_index("tp")
    grp_i = lax.axis_index("grp")
    core = lax.rem(tp_i, 2)
    chip = tp_i // 2
    other = 1 - core
    partner = {"tp": chip * 2 + other}

    def peer(dy):
        return lax.rem(chip + dy, chips)

    def peer_id(dy):
        return {"tp": peer(dy) * 2 + core}

    def share(slot):
        return pl.ds(pl.multiple_of(slot * chan, 16), chan)

    names = ["taps", "wkt", "wup", "wdn", "q", "wko"]
    sources = [
        (taps_hbm, tapst),
        (wkt_hbm, wkt),
        (wup_hbm, wup),
        (wdn_hbm, wdn),
        (q_hbm, qbuf),
        (wko_hbm, wko),
    ]
    loads = {
        name: pltpu.make_async_copy(src, dst, w_sem.at[i])
        for i, (name, (src, dst)) in enumerate(zip(names, sources))
    }
    own_x = [
        pltpu.make_async_copy(x_hbm.at[order[pos]], xg.at[pos, share(tp_i)], w_sem.at[6 + pos])
        for pos in range(places)
    ]
    for c in own_x:
        c.start()
    for name in names:
        loads[name].start()

    barrier = pltpu.get_barrier_semaphore()
    pl.semaphore_signal(barrier, inc=1, device_id=partner, device_id_type=MESH)
    for dy in range(1, chips):
        pl.semaphore_signal(barrier, inc=1, device_id=peer_id(dy), device_id_type=MESH)

    @pl.when(grp_i > 0)
    def _():
        pl.semaphore_signal(barrier, inc=1, device_id={"grp": grp_i - 1}, device_id_type=MESH)

    @pl.when(grp_i < grp_n - 1)
    def _():
        pl.semaphore_signal(barrier, inc=1, device_id={"grp": grp_i + 1}, device_id_type=MESH)

    neighbours = jnp.where(grp_i > 0, 1, 0) + jnp.where(grp_i < grp_n - 1, 1, 0)
    pl.semaphore_wait(barrier, chips + neighbours)

    def rows(ch):
        return pl.ds(ch * rc, rc)

    def x_copy(pos, dy):
        return pltpu.make_async_remote_copy(
            src_ref=x_hbm.at[order[pos]],
            dst_ref=xg.at[pos, share(tp_i)],
            send_sem=x_ssem.at[pos, dy],
            recv_sem=x_rsem.at[pos, dy],
            device_id=peer_id(dy) if dy else partner,
            device_id_type=MESH,
        )

    def x_pass(pos, dy):
        slot = lax.rem(chip - dy + chips, chips) * 2 + core
        return pltpu.make_async_remote_copy(
            src_ref=xg.at[pos, share(slot)],
            dst_ref=xg.at[pos, share(slot)],
            send_sem=xp_ssem.at[pos, dy],
            recv_sem=xp_rsem.at[pos, dy],
            device_id=partner,
            device_id_type=MESH,
        )

    def x_forward(pos):
        for dy in range(1, chips):
            x_copy(pos, dy).wait_recv()
            x_pass(pos, dy).start()

    for pos in range(places):
        for dy in list(range(1, chips)) + [0]:
            x_copy(pos, dy).start()

    kv_cols = kvt.shape[1]
    step = 2 * HD

    def tap_rows(pos):
        taps[pos * tile : (pos + 1) * tile, :] = tapst[order[pos]].T

    tap_blocks = kv_cols // step

    def tap_product(low, high):
        def body(at, carry):
            block = lax.rem(at * kv_heads, tap_blocks) + at * kv_heads // tap_blocks
            cols = pl.ds(pl.multiple_of(block * step, step), step)
            kvt[:, cols] = jnp.dot(taps[...], wkt[:, cols], preferred_element_type=F32)
            return carry

        lax.fori_loop(low, high, body, 0)

    units = hidden.shape[1]

    def layer_norm(pos):
        own_x[pos].wait()
        x_copy(pos, 0).wait_recv()
        for dy in range(1, chips):
            x_pass(pos, dy).wait_recv()
        blocks = [slice(b * HD, (b + 1) * HD) for b in range(depth // HD)]
        total = jnp.zeros((8, tile), F32)
        for b in blocks:
            values = xg[pos, b, :].astype(F32)
            total = total + jnp.sum(values.reshape(HD // 8, 8, tile), axis=0)
        average = jnp.sum(total, axis=0, keepdims=True) / depth
        square = jnp.zeros((8, tile), F32)
        for b in blocks:
            centered = xg[pos, b, :].astype(F32) - average
            square = square + jnp.sum((centered * centered).reshape(HD // 8, 8, tile), axis=0)
        factor = lax.rsqrt(jnp.sum(square, axis=0, keepdims=True) / depth + epsilon)
        for b in blocks:
            scaled = ((xg[pos, b, :].astype(F32) - average) * factor).T
            normed[:, b] = (scaled * gain_ref[b].reshape(1, HD) + bias_ref[b].reshape(1, HD)).astype(
                BF16
            )

    def up(pos):
        if pos == 0:
            loads["wup"].wait()
        for j in range(0, units, 256):
            cols = slice(j, min(j + 256, units))
            pre = jnp.dot(normed[...], wup[:, cols], preferred_element_type=F32)
            pre = pre + bup_ref[cols].reshape(1, -1)
            hidden[:, cols] = (0.5 * pre * (1.0 + lax.erf(pre * (0.5**0.5)))).astype(BF16)

    def down(pos):
        if pos == 0:
            loads["wdn"].wait()
        terms = jnp.dot(hidden[...], wdn[...], preferred_element_type=F32).astype(BF16).T
        for t in range(tp_n):
            m_send[pos, t % 2, t // 2] = terms[t * chan : (t + 1) * chan, :]
        start_l1((0, pos))

    def buffers(stage):
        which, at = stage
        if which == 0:
            return (b.at[at] for b in (m_send, m_r1, m_s2, m_r2))
        return (b.at[at] for b in (k_send, k_r1, k_s2, k_r2))

    def number(stage):
        which, at = stage
        return at if which == 0 else places + at

    def l1(stage, dy):
        send, r1, _, _ = buffers(stage)
        y = peer(dy)
        return pltpu.make_async_remote_copy(
            src_ref=send.at[other, y],
            dst_ref=r1.at[y],
            send_sem=l1_ssem.at[number(stage), dy],
            recv_sem=l1_rsem.at[number(stage), dy],
            device_id=partner,
            device_id_type=MESH,
        )

    def start_l1(stage):
        for dy in list(range(1, chips)) + [0]:
            l1(stage, dy).start()

    def l2(stage, dy):
        _, _, s2, r2 = buffers(stage)
        return pltpu.make_async_remote_copy(
            src_ref=s2.at[dy - 1],
            dst_ref=r2.at[dy - 1],
            send_sem=l2_ssem.at[number(stage), dy - 1],
            recv_sem=l2_rsem.at[number(stage), dy - 1],
            device_id=peer_id(dy),
            device_id_type=MESH,
        )

    def level2(stage):
        send, r1, s2, _ = buffers(stage)
        for dy in range(1, chips):
            y = peer(dy)
            l1(stage, dy).wait_recv()
            s2[dy - 1] = (send[core, y].astype(F32) + r1[y].astype(F32)).astype(BF16)
            l2(stage, dy).start()

    def summed(stage):
        send, r1, _, r2 = buffers(stage)
        l1(stage, 0).wait_recv()
        total = send[core, chip].astype(F32) + r1[chip].astype(F32)
        for dy in range(1, chips):
            l2(stage, dy).wait_recv()
            total = total + r2[dy - 1].astype(F32)
        return total

    def encode(pos):
        here = summed((0, pos)) + xg[pos, share(tp_i), :].astype(F32)
        encoded[pos * tile : (pos + 1) * tile, :] = (
            here.T + bdn_ref[...].reshape(1, chan)
        ).astype(BF16)

    def project(h, ch):
        if h == 0 and ch == 0:
            loads["wko"].wait()
        at = h * nch + ch
        for t in range(tp_n):
            start = (t * KVH // tp_n + h) * step
            cols = slice(start, start + step)
            k_send[at, t % 2, t // 2] = (
                jnp.dot(encoded[rows(ch), :], wko[:, cols], preferred_element_type=F32)
                + kvt[rows(ch), cols]
            ).astype(BF16)
        start_l1((1, at))

    def finish(h, ch):
        total = summed((1, h * nch + ch))
        key = total[:, :HD]
        square = jnp.mean(key * key, axis=-1, keepdims=True)
        key = (key * lax.rsqrt(square + epsilon) * kgain_ref[...].reshape(1, HD)).astype(BF16)
        value = total[:, HD:].astype(BF16)
        for p in range(per):
            pos = ch * per + p
            at = order[pos] * grp_n + grp_i
            kvs[h][at, :, :HD] = key[p * tile : (p + 1) * tile]
            kvs[h][at, :, HD:] = value[p * tile : (p + 1) * tile]
        for pos, way in travels(h):
            if pos // per == ch:
                z_start(h, pos, way, 0)

    def reaches_up(index, q):
        return (index >= REQ_G * q) & (index >= total_tiles - CAP * (grp_n - q))

    def reaches_down(index, q):
        return (index < total_tiles - REQ_G * (grp_n - 1 - q)) & (index < CAP * (q + 1))

    def z_copy(h, pos, way, k):
        block = jnp.clip(grp_i - k if way == 0 else grp_i + k, 0, grp_n - 1)
        at = order[pos] * grp_n + block
        return pltpu.make_async_remote_copy(
            src_ref=kvs[h].at[at],
            dst_ref=kvs[h].at[at],
            send_sem=z_ssem.at[h, way, pos, k],
            recv_sem=z_rsem.at[h, way, pos, k],
            device_id={"grp": grp_i + 1 if way == 0 else grp_i - 1},
            device_id_type=MESH,
        )

    def z_sends(pos, way, k):
        base = order[pos] * grp_n
        if way == 0:
            return (grp_i - k >= 0) & (grp_i < grp_n - 1) & reaches_up(base + grp_i - k, grp_i + 1)
        return (grp_i + k <= grp_n - 1) & (grp_i > 0) & reaches_down(base + grp_i + k, grp_i - 1)

    def z_gets(pos, way, k):
        base = order[pos] * grp_n
        if way == 0:
            return (grp_i - k - 1 >= 0) & reaches_up(base + grp_i - k - 1, grp_i)
        return (grp_i + k + 1 <= grp_n - 1) & reaches_down(base + grp_i + k + 1, grp_i)

    def z_start(h, pos, way, k):
        @pl.when(z_sends(pos, way, k))
        def _():
            z_copy(h, pos, way, k).start()

    def chunks(h):
        return range(nch) if h == 0 else range(nch - 1, -1, -1)

    def travels(h):
        found = []
        for ch in chunks(h):
            here = list(range(ch * per, (ch + 1) * per))
            up_way = sorted(here, key=lambda pos: -order[pos])
            down_way = sorted(here, key=lambda pos: order[pos])
            for p in range(per):
                found += [(up_way[p], 0), (down_way[p], 1)]
        return found

    def z_hop(h, k, low=0, high=None):
        for pos, way in travels(h)[low:high]:

            @pl.when(z_gets(pos, way, k))
            def _(pos=pos, way=way):
                z_copy(h, pos, way, k).wait_recv()

            if k + 1 < grp_n - 1:
                z_start(h, pos, way, k + 1)

    text_rows = qbuf.shape[0]
    q_heads = qbuf.shape[1] // HD
    per_kv = q_heads // kv_heads
    half = text_rows // REQ_G
    window = min(MAXT, total_tiles)

    offset = jnp.int32(0)
    tiles = [jnp.int32(0), jnp.int32(0)]
    texts = [jnp.int32(0), jnp.int32(0)]
    seen = jnp.int32(0)
    for r in range(owner_ref.shape[0]):
        own = owner_ref[r] == grp_i
        offset = offset + jnp.where(owner_ref[r] < grp_i, tiles_ref[r], 0)
        for i in range(REQ_G):
            here = own & (seen == i)
            tiles[i] = jnp.where(here, tiles_ref[r], tiles[i])
            texts[i] = jnp.where(here, text_ref[r], texts[i])
        seen = seen + own.astype(jnp.int32)

    def head_cols(qh):
        return pl.ds(pl.multiple_of(qh * HD, HD), HD)

    def norm_queries(low, high):
        def body(qh, carry):
            query = qbuf[:, head_cols(qh)].astype(F32)
            square = jnp.mean(query * query, axis=-1, keepdims=True)
            gain = qgain_ref[...].reshape(1, HD) * (LOG2E / float(HD) ** 0.5)
            query = query * lax.rsqrt(square + epsilon) * gain
            qrows[...] = query
            qnorm[0, :, head_cols(qh)] = query[:half].astype(BF16)
            qnorm[1, :, head_cols(qh)] = qrows[pl.ds(texts[0], half), :].astype(BF16)
            return carry

        lax.fori_loop(low, high, body, 0)

    def windows(h):
        for i in range(REQ_G):
            low = offset if i == 0 else offset + tiles[0]
            start = jnp.minimum(low, total_tiles - window)
            here = kvs[h][pl.ds(start, window)].reshape(window * tile, 2 * HD)
            row = lax.broadcasted_iota(jnp.int32, (window * tile, HD), 0) + start * tile
            valid = (row >= low * tile) & (row < (low + tiles[i]) * tile)
            kwin[i] = jnp.where(valid, here[:, :HD].astype(F32), 0.0).astype(BF16)
            vwin[i, :, :HD] = jnp.where(valid, here[:, HD:].astype(F32) * V_SCALE, 0.0).astype(BF16)
            vwin[i, :, HD:] = jnp.where(valid, V_SCALE, 0.0).astype(BF16)

    def out_copy(pair):
        cols = pl.ds(pl.multiple_of(pair * 2 * HD, HD), 2 * HD)
        return pltpu.make_async_copy(obuf.at[pair], out_ref.at[:, cols], o_sem.at[pair])

    def attend(low, high):
        row = lax.broadcasted_iota(jnp.int32, (half, 1), 0)
        both = texts[0] + texts[1]
        first = row < texts[0]
        top, bottom = row < both, row + half < both

        def request(qh, i):
            scores = lax.dot_general(
                qnorm[i, :, head_cols(qh)],
                kwin[i],
                (((1,), (1,)), ((), ())),
                preferred_element_type=F32,
            )
            weights = jnp.exp2(scores).astype(BF16)
            result = jnp.dot(weights, vwin[i], preferred_element_type=F32)
            return result[:, :HD] / result[:, HD:]

        def body(pair, carry):
            for slot in range(2):
                qh = pair * 2 + slot
                orows[slot, half : 2 * half] = request(qh, 1)
                moved = orows[slot, pl.ds(half - texts[0], text_rows)]
                mine = request(qh, 0)
                inside = slice(slot * HD, (slot + 1) * HD)
                obuf[pair, :half, inside] = jnp.where(
                    first, mine, jnp.where(top, moved[:half], 0.0)
                ).astype(BF16)
                obuf[pair, half:, inside] = jnp.where(bottom, moved[half:], 0.0).astype(BF16)
            out_copy(pair).start()
            return carry

        lax.fori_loop(low, high, body, 0)

    loads["taps"].wait()
    for pos in range(places):
        tap_rows(pos)
    loads["wkt"].wait()

    ready = tap_blocks // kv_heads
    tapped = tap_blocks * 5 // 8
    tap_product(0, tapped)
    x_forward(0)
    for pos in range(places):
        layer_norm(pos)
        up(pos)
        if pos > 0:
            level2((0, pos - 1))
        if pos + 1 < places:
            x_forward(pos + 1)
        down(pos)
    if tapped < ready:
        tap_product(tapped, ready)
        tapped = ready
    level2((0, places - 1))

    def encode_chunk(ch):
        for pos in range(ch * per, (ch + 1) * per):
            encode(pos)

    stages = [(h, ch) for h in range(kv_heads) for ch in range(nch)]
    encode_chunk(0)
    project(0, 0)
    level2((1, 0))
    if tapped < tap_blocks:
        tap_product(tapped, tap_blocks)
    pending = [(h, ch) for h in range(1, kv_heads) for ch in chunks(h)]
    for ch in range(1, nch):
        encode_chunk(ch)
        project(0, ch)
    for later in pending:
        project(*later)
    for ch in range(1, nch):
        level2((1, ch))
    finish(0, 0)
    for h, ch in pending:
        level2((1, h * nch + ch))
    loads["q"].wait()
    norm_queries(0, q_heads)
    z_hop(0, 0, 0, 2)
    for ch in range(1, nch):
        finish(0, ch)
    last = grp_n - 2
    for h in range(kv_heads):
        if h == 0:
            coming = pending[:nch]
            for k in range(last):
                z_hop(0, k, 2 if k == 0 else 0)
                if coming:
                    finish(*coming.pop(0))
            while coming:
                finish(*coming.pop(0))
        z_hop(h, last)
        windows(h)
        base = h * per_kv
        if h + 1 < kv_heads:
            parts = last + 1
            edges = [(base + per_kv * p // parts) // 2 for p in range(parts + 1)]
            for k in range(parts):
                attend(edges[k], edges[k + 1])
                if k < last:
                    z_hop(h + 1, k)
        else:
            attend(base // 2, (base + per_kv) // 2)

    for pos in range(places):
        for dy in range(chips):
            x_copy(pos, dy).wait_send()
        for dy in range(1, chips):
            x_pass(pos, dy).wait_send()
    for stage in [(0, pos) for pos in range(places)] + [(1, j) for j in range(len(stages))]:
        for dy in range(chips):
            l1(stage, dy).wait_send()
        for dy in range(1, chips):
            l2(stage, dy).wait_send()
    for h in range(kv_heads):
        for pos in range(places):
            for k in range(grp_n - 1):
                for way in range(2):

                    @pl.when(z_sends(pos, way, k))
                    def _(h=h, pos=pos, way=way, k=k):
                        z_copy(h, pos, way, k).wait_send()
    for pair in range(q_heads // 2):
        out_copy(pair).wait()


def local(
    x_in,
    taps,
    ln_gain,
    ln_bias,
    w_up,
    b_up,
    w_down,
    b_down,
    kv_w_out,
    kv_w_taps,
    k_gain,
    q_gain,
    queries,
    tiles_per_request,
    owner,
    text_per_request,
):
    grp_n = lax.axis_size("grp")
    tp_n = lax.axis_size("tp")
    chips = tp_n // 2
    places, _, tile, chan = x_in.shape
    n = places * tile
    nch = 2 if places % 2 == 0 else 1
    rc = n // nch
    depth, units = w_up.shape
    tap_share, kv_cols = kv_w_taps.shape
    kv_heads = max(1, KVH // tp_n)
    width = 2 * HD
    stages = kv_heads * nch
    text_rows, query_width = queries.shape
    half = text_rows // REQ_G
    window = min(MAXT, places * grp_n) * tile
    any_spec = pl.BlockSpec(memory_space=pl.ANY)
    vmem_spec = pl.BlockSpec(memory_space=pltpu.VMEM)
    smem_spec = pl.BlockSpec(memory_space=pltpu.SMEM)
    dma = pltpu.SemaphoreType.DMA
    return pl.pallas_call(
        functools.partial(fused_kernel, (tp_n, grp_n, nch, chan, kv_heads)),
        name="fused",
        out_shape=pltpu.VMEM(queries.shape, BF16),
        in_specs=[
            any_spec,
            any_spec,
            vmem_spec,
            vmem_spec,
            any_spec,
            vmem_spec,
            any_spec,
            vmem_spec,
            any_spec,
            any_spec,
            vmem_spec,
            vmem_spec,
            any_spec,
            smem_spec,
            smem_spec,
            smem_spec,
        ],
        out_specs=any_spec,
        scratch_shapes=[
            pltpu.VMEM((places, depth, tile), BF16),
            pltpu.VMEM((tile, depth), BF16),
            pltpu.VMEM((tile, units), BF16),
            pltpu.VMEM((places, tap_share, tile), BF16),
            pltpu.VMEM((n, tap_share), BF16),
            pltpu.VMEM(w_up.shape, BF16),
            pltpu.VMEM(w_down.shape, BF16),
            pltpu.VMEM(kv_w_out.shape, BF16),
            pltpu.VMEM(kv_w_taps.shape, BF16),
            pltpu.VMEM((n, kv_cols), F32),
            pltpu.VMEM((n, chan), BF16),
            pltpu.VMEM((places, 2, chips, chan, tile), BF16),
            pltpu.VMEM((places, chips, chan, tile), BF16),
            pltpu.VMEM((places, chips - 1, chan, tile), BF16),
            pltpu.VMEM((places, chips - 1, chan, tile), BF16),
            pltpu.VMEM((stages, 2, chips, rc, width), BF16),
            pltpu.VMEM((stages, chips, rc, width), BF16),
            pltpu.VMEM((stages, chips - 1, rc, width), BF16),
            pltpu.VMEM((stages, chips - 1, rc, width), BF16),
            pltpu.VMEM((REQ_G, window, HD), BF16),
            pltpu.VMEM((REQ_G, window, 2 * HD), BF16),
            pltpu.VMEM((text_rows, query_width), BF16),
            pltpu.VMEM((REQ_G, half, query_width), BF16),
            pltpu.VMEM((text_rows, HD), F32),
            pltpu.VMEM((2, half + text_rows, HD), F32),
            pltpu.VMEM((query_width // (2 * HD), text_rows, 2 * HD), BF16),
        ]
        + [pltpu.VMEM((places * grp_n, tile, width), BF16) for _ in range(kv_heads)]
        + [
            dma((6 + places,)),
            dma((places, chips)),
            dma((places, chips)),
            dma((places, chips)),
            dma((places, chips)),
            dma((places + stages, chips)),
            dma((places + stages, chips)),
            dma((places + stages, chips - 1)),
            dma((places + stages, chips - 1)),
            dma((kv_heads, 2, places, grp_n - 1)),
            dma((kv_heads, 2, places, grp_n - 1)),
            dma((query_width // (2 * HD),)),
        ],
        compiler_params=pltpu.CompilerParams(
            collective_id=0, has_side_effects=True, vmem_limit_bytes=VMEM_BYTES
        ),
    )(
        jnp.transpose(x_in, (0, 1, 3, 2)).reshape(places, chan, tile),
        jnp.transpose(taps, (0, 1, 3, 2)).reshape(places, tap_share, tile),
        ln_gain,
        ln_bias,
        w_up,
        b_up,
        w_down,
        b_down,
        kv_w_out,
        kv_w_taps,
        k_gain,
        q_gain,
        queries,
        tiles_per_request,
        owner,
        text_per_request,
    )


def solution(mesh):
    in_specs = (
        P(None, ("rep", "grp"), None, "tp"),
        P(None, ("rep", "grp"), None, "tp"),
        P(),
        P(),
        P(None, "tp"),
        P("tp"),
        P("tp", None),
        P("tp"),
        P("tp", None),
        P("tp", None),
        P(),
        P(),
        P(("rep", "grp"), "tp"),
        P("rep"),
        P("rep"),
        P("rep"),
    )
    out_specs = P(("rep", "grp"), "tp")
    return jax.shard_map(local, mesh=mesh, in_specs=in_specs, out_specs=out_specs, check_vma=False)
```
